32 devices in a mesh: group: 4 (over y, core), member: 8 (over z, x).
Axes of the slice: x: 2, y: 2, z: 4, core: 2. Of those that a mesh axis runs over, the one named last changes fastest.
Arguments:
- position: float32 [3, 262144], P(None, ('group', 'member')), may hold values from -6 to 6
- velocity: float32 [3, 262144], P(None, ('group', 'member')), may hold values from -6 to 6
- mass: float32 [262144], P(('group', 'member')), may hold values from 0.0009765625 to 0.0078125
- neighbours: int32 [2048, 4], P(('group', 'member')), may hold values from 0 to 71
- list_length: int32 [2048], P(('group', 'member')), may hold values from 1 to 4
- let_list: int32 [32, 8], P(('group', 'member')), may hold values from 0 to 63
- cell_list: int32 [32, 32], P(('group', 'member')), may hold values from 0 to 511
- destination: int32 [2, 2048], P(None, ('group', 'member')), may hold values from 0 to 7, as said below
Outputs:
- final_position: float32 [3, 262144], P(None, ('group', 'member'))
- final_velocity: float32 [3, 262144], P(None, ('group', 'member'))
- final_mass: float32 [262144], P(('group', 'member'))
The draws below stay inside these ranges and needn't reach their ends.
Inputs may be any that keep to these rules, and one draw needn't show every extreme that they name: `neighbours`: index into the pool of the block's device: its 64 own blocks, then one block from each member of its group in member order. Only the first list_length entries of a block's list are used. `destination`: in each step and group, all devices move the block in slot b the same number of places along member, wrapping around, so every device receives exactly one block for each slot; a device sends at most 8 blocks to one device, and in every step and group some device sends exactly that many to one device.
All inputs are finite; a program needn't handle non-finite values.
Results may differ from the reference program's by a relative error of at most 0.0003.
Values sent between devices are 32-bit elements; how exact they have to be, the bound alone decides.
A program may use at most 64 MiB of HBM per device.

```python
import math
import jax
import jax.numpy as jnp
from jax import lax

BLOCK = 128
NB = 64
CELL = 16
LIST = 4
MSEND = 32
PDEV = 8192
BLOCKS = 2048
TOTAL = 262144
POOL = 72
MCAP = 8
NCELL = 512
N_GROUP = 4
N_MEMBER = 8


def draw_destination(key, part):
    base_key = jax.random.fold_in(key, 11)
    keys_all = jax.random.split(base_key, 2 * N_GROUP)

    def offsets_for(one_key):
        first_key, second_key = jax.random.split(one_key)
        slot_order = jax.random.permutation(first_key, NB)
        chosen_offsets = jax.random.permutation(second_key, N_MEMBER)
        return chosen_offsets[slot_order // MCAP]
    offsets = jax.vmap(offsets_for)(keys_all).reshape(2, N_GROUP, 1, NB)
    members = jnp.arange(N_MEMBER, dtype=jnp.int32).reshape(1, 1, N_MEMBER, 1)
    return ((members + offsets) % N_MEMBER).reshape(2, N_GROUP * N_MEMBER * NB).astype(jnp.int32)


def draw_position(key, part):
    device_count = N_GROUP * N_MEMBER
    side = int(math.ceil(device_count ** (1.0 / 3.0) - 1e-09))
    if side ** 3 < device_count:
        side = side + 1
    columns = jnp.arange(TOTAL, dtype=jnp.int32)
    device = columns // PDEV
    lattice = jnp.stack([device % side, device // side % side, device // (side * side)], axis=0).astype(jnp.float32)
    centre = -3.4 + 6.8 * (lattice + 0.5) / side
    cell_key, point_key = jax.random.split(jax.random.fold_in(key, 23))
    cell_count = TOTAL // CELL
    cell_offset = jnp.clip(0.25 * jax.random.normal(cell_key, (3, cell_count), jnp.float32), -1.0, 1.0)
    point_offset = jnp.clip(0.05 * jax.random.normal(point_key, (3, TOTAL), jnp.float32), -0.2, 0.2)
    cell_spread = jnp.repeat(cell_offset, CELL, axis=1)
    return (centre + cell_spread + point_offset).astype(jnp.float32)


def set_ends(values, stream_key, low, largest):
    longest = values.shape.index(max(values.shape))
    spots = []
    for shift in (0, 1):
        where = [jax.random.randint(jax.random.fold_in(stream_key, axis), (), 0, length) for axis, length in enumerate(values.shape)]
        where[longest] = (where[longest] + shift) % values.shape[longest]
        spots.append(tuple(where))
    return values.at[spots[0]].set(low).at[spots[1]].set(largest)


def block_levels(key, extent, pieces, least, largest):
    level = 1.0
    for dim, parts in pieces:
        steps = jax.random.uniform(jax.random.fold_in(jax.random.fold_in(key, 6), dim), (parts,), jnp.float32, least / len(pieces), largest / len(pieces))
        level = level * jnp.repeat(jnp.exp(steps), extent[dim] // parts).reshape((-1,) + (1,) * (len(extent) - 1 - dim))
    return level


def bell_draw(own_key, shape, width, reach, pieces=(), kind=jnp.bfloat16):
    gain = block_levels(own_key, shape, pieces, -0.22, 0.18) if pieces else 1.0
    drawn = jax.random.normal(own_key, shape, jnp.float32) * width * gain
    return jnp.minimum(jnp.maximum(drawn, -reach), reach).astype(kind)


def setup_inputs(seed: int = 0) -> dict:
    keys = jax.random.split(jax.random.key(seed), 9)
    return {
        "position": draw_position(jax.random.fold_in(keys[8], 71), 0),
        "velocity": bell_draw(keys[1], (3, TOTAL), 1.0, 6.0, ((1, 32),), jnp.float32),
        "mass": jnp.clip(jnp.exp(math.log(0.0078125) - 2.0794415 * jax.random.uniform(keys[2], (TOTAL,), jnp.float32) ** block_levels(keys[2], (TOTAL,), ((0, 32),), -0.2, 0.2)), 0.0009765625, 0.0078125),
        "neighbours": set_ends(jax.random.randint(keys[3], (BLOCKS, LIST), 0, POOL), jax.random.fold_in(keys[3], 1), 0, POOL - 1).astype(jnp.int32),
        "list_length": set_ends(jax.random.randint(keys[4], (BLOCKS,), max(1, LIST // 4), LIST + 1), jax.random.fold_in(keys[4], 1), max(1, LIST // 4), LIST).astype(jnp.int32),
        "let_list": set_ends(jax.random.randint(keys[5], (N_GROUP * N_MEMBER, N_MEMBER), 0, NB), jax.random.fold_in(keys[5], 1), 0, NB - 1).astype(jnp.int32),
        "cell_list": set_ends(jax.random.randint(keys[6], (N_GROUP * N_MEMBER, MSEND), 0, NCELL), jax.random.fold_in(keys[6], 1), 0, NCELL - 1).astype(jnp.int32),
        "destination": draw_destination(jax.random.fold_in(keys[8], 71), 0),
    }


SOFTENING = 0.01
TIMESTEP = 0.1

def pull_toward(targets, sources):
    offset = sources[:3, :, None] - targets[:, None, :]
    radius_sq = lax.optimization_barrier(jnp.sum(offset * offset, axis=0)) + SOFTENING
    inverse = lax.rsqrt(radius_sq)
    weight = sources[3][:, None] * inverse * inverse * inverse
    return lax.optimization_barrier(jnp.sum(offset * weight[None], axis=1))

def all_forces(halfway, mass, neighbours, list_length, let_list, cell_list):
    layout = (N_GROUP, N_MEMBER, NB, BLOCK)
    coords = halfway.reshape((3,) + layout)
    weights = mass.reshape((1,) + layout)
    blocks = jnp.concatenate([coords, weights], axis=0)
    remote_index = let_list.reshape(N_GROUP, N_MEMBER, N_MEMBER)
    sent = jnp.take_along_axis(blocks, remote_index[None, :, :, :, None], axis=3)
    received = jnp.swapaxes(sent, 2, 3)
    source_pool = jnp.concatenate([blocks, received], axis=3)
    cell_mass = weights[0].reshape(N_GROUP, N_MEMBER, NB * BLOCK // CELL, CELL).sum(-1)
    cell_centre = (coords * weights).reshape(3, N_GROUP, N_MEMBER, NB * BLOCK // CELL, CELL).sum(-1) / cell_mass
    cells = jnp.concatenate([cell_centre, cell_mass[None]], axis=0)
    chosen_cells = jnp.take_along_axis(cells, cell_list.reshape(1, N_GROUP, N_MEMBER, MSEND), axis=3)
    lists = neighbours.reshape(N_GROUP, N_MEMBER, NB, LIST)
    lengths = list_length.reshape(N_GROUP, N_MEMBER, NB)

    def per_device(device):
        group_here = device // N_MEMBER
        member_here = device % N_MEMBER
        targets = coords[:, group_here, member_here]
        pool_here = source_pool[:, group_here, member_here]
        far_cells = chosen_cells[:, :, member_here]
        keep_group = (jnp.arange(N_GROUP, dtype=jnp.int32) != group_here).astype(far_cells.dtype)
        far_sources = jnp.concatenate([far_cells[:3], (far_cells[3] * keep_group[:, None])[None]], axis=0).reshape(4, -1)

        def one_block(block_targets, block_list, block_length):
            chosen = pool_here[:, block_list]
            live = (jnp.arange(LIST, dtype=jnp.int32) < block_length).astype(chosen.dtype)
            sources = jnp.concatenate([chosen[:3], (chosen[3] * live[:, None])[None]], axis=0).reshape(4, -1)
            return pull_toward(block_targets, sources) + pull_toward(block_targets, far_sources)
        return jax.vmap(one_block, in_axes=(1, 0, 0), out_axes=1)(targets, lists[group_here, member_here], lengths[group_here, member_here])
    result = lax.map(per_device, jnp.arange(N_GROUP * N_MEMBER, dtype=jnp.int32))
    return jnp.moveaxis(result, 1, 0).reshape(3, -1)

def migrate(position, velocity, mass, target_flat):
    block_state = jnp.concatenate([position, velocity, mass[None]], axis=0).reshape(7, N_GROUP, N_MEMBER, NB, BLOCK)
    target_member = target_flat.reshape(N_GROUP, N_MEMBER, NB)
    group_rows = jnp.arange(N_GROUP, dtype=jnp.int32)[:, None, None]
    slot_rows = jnp.arange(NB, dtype=jnp.int32)[None, None, :]
    moved_state = jnp.zeros_like(block_state).at[:, group_rows, target_member, slot_rows].set(block_state)
    flattened = moved_state.reshape(7, -1)
    return (flattened[0:3], flattened[3:6], flattened[6])

def reference(position, velocity, mass, neighbours, list_length, let_list, cell_list, destination):
    for turn_index in range(2):
        halfway = position + 0.5 * TIMESTEP * velocity
        acceleration = all_forces(halfway, mass, neighbours, list_length, let_list, cell_list)
        velocity = velocity + TIMESTEP * acceleration
        position = halfway + 0.5 * TIMESTEP * velocity
        position, velocity, mass = migrate(position, velocity, mass, destination[turn_index])
    return (position, velocity, mass)
```

```python
import functools

import jax
import jax.numpy as jnp
from jax import lax
from jax.experimental import pallas as pl
from jax.experimental.pallas import tpu as pltpu
from jax.sharding import PartitionSpec as P

BLOCK = 128
CELL = 16
SOFTENING = 0.01
TIMESTEP = 0.1
ROWS = 8
FEATS = 64
HALF = 0.5 * TIMESTEP
GATHERED = 16


def parts_of(value):
    high = value.astype(jnp.bfloat16).astype(jnp.float32)
    rest = value - high
    middle = rest.astype(jnp.bfloat16).astype(jnp.float32)
    return high, middle, rest - middle


def rows_of(shape):
    return lax.broadcasted_iota(jnp.int32, shape, 0)


def source_features(block):
    row = rows_of(block.shape)
    mass = block[3:4]
    square = jnp.sum(jnp.where(row < 3, block * block, 0.0), axis=0, keepdims=True)
    tail = jnp.where(row == 3, square, jnp.where(row == 4, 1.0, 0.0))
    high, middle, low = parts_of(jnp.where(row < 3, block, tail))
    columns = jnp.concatenate([high, high, high, middle, middle, middle, low, low], axis=0)
    weighted = jnp.where(row < 3, block * mass, jnp.where(row == 3, mass, 0.0))
    heavy, light, least = [part[0:4] for part in parts_of(weighted)]
    moments = jnp.concatenate([heavy, light, least, jnp.zeros_like(least)], axis=0)
    return jnp.transpose(columns).astype(jnp.bfloat16), moments.astype(jnp.bfloat16)


def target_features(block):
    row = rows_of(block.shape)
    square = jnp.sum(jnp.where(row < 3, block * block, 0.0), axis=0, keepdims=True)
    tail = jnp.where(row == 3, 1.0, jnp.where(row == 4, square + SOFTENING, 0.0))
    high, middle, low = parts_of(jnp.where(row < 3, -2.0 * block, tail))
    rows = jnp.concatenate([high, middle, low, high, middle, low, high, middle], axis=0)
    return rows.astype(jnp.bfloat16)


def weights_of(radius_sq):
    inverse = lax.rsqrt(radius_sq)
    return (inverse * inverse * inverse).astype(jnp.bfloat16)


def fold(sums):
    pair = sums[0:8] + sums[8:16]
    return pair[0:4] + pair[4:8]


def kernel(
    sizes,
    ints,
    position,
    velocity,
    mass,
    out_position,
    out_velocity,
    out_mass,
    half,
    speed,
    columns,
    moments,
    targets,
    weights,
    far_columns,
    far_moments,
    let_out,
    let_in,
    cell_out,
    cell_in,
    move_out,
    move_in,
    let_send,
    let_recv,
    cell_send,
    cell_recv,
    move_send,
    move_recv,
):
    blocks, entries, members, groups, capacity, publish = sizes
    slots = members * capacity
    chunks = far_columns.shape[0]
    per_chunk = groups // chunks
    lengths_at = blocks * entries
    let_at = lengths_at + blocks
    cells_at = let_at + members
    order_at = cells_at + publish
    slot_at = order_at + 2 * slots
    group, member = lax.axis_index("group"), lax.axis_index("member")

    def peer(distance):
        return {"member": lax.rem(member + distance, members)}

    def group_peer(distance):
        return {"group": lax.rem(group + distance, groups)}

    mesh_id = pl.DeviceIdType.MESH
    barrier = pltpu.get_barrier_semaphore()
    for distance in range(1, members):
        pl.semaphore_signal(barrier, inc=1, device_id=peer(distance), device_id_type=mesh_id)
    for distance in range(1, groups):
        pl.semaphore_signal(barrier, inc=1, device_id=group_peer(distance), device_id_type=mesh_id)

    def let_copy(turn, distance):
        return pltpu.make_async_remote_copy(
            src_ref=let_out.at[turn, distance],
            dst_ref=let_in.at[turn, distance],
            send_sem=let_send.at[turn, distance],
            recv_sem=let_recv.at[turn, distance],
            device_id=peer(distance),
            device_id_type=mesh_id,
        )

    def cell_copy(turn, distance):
        return pltpu.make_async_remote_copy(
            src_ref=cell_out.at[turn],
            dst_ref=cell_in.at[turn, distance],
            send_sem=cell_send.at[turn, distance],
            recv_sem=cell_recv.at[turn, distance],
            device_id=group_peer(distance),
            device_id_type=mesh_id,
        )

    def move_copy(turn, distance):
        return pltpu.make_async_remote_copy(
            src_ref=move_out.at[turn, distance],
            dst_ref=move_in.at[turn, distance],
            send_sem=move_send.at[turn, distance],
            recv_sem=move_recv.at[turn, distance],
            device_id=peer(distance),
            device_id_type=mesh_id,
        )

    def arrived(turn, block):
        slot = ints[slot_at + turn * blocks + block]
        return move_in[turn, slot // capacity, slot % capacity]

    together = max(1, min(members, GATHERED // capacity))
    while members % together:
        together -= 1
    once = jnp.minimum(member + 1, 1)

    def distance_at(index):
        swing = (index + 1) // 2
        away = members // 2 + jnp.where(index % 2 == 1, -swing, swing)
        return jnp.where(index == members - 1, 0, away)

    speed[...] = jnp.zeros_like(speed)
    half[...] = jnp.zeros_like(half)
    row = rows_of((ROWS, BLOCK))
    lane = lax.broadcasted_iota(jnp.int32, (ROWS, BLOCK), 1)

    for turn in range(2):

        def load_block(block, _):
            at = pl.ds(pl.multiple_of(block * BLOCK, BLOCK), BLOCK)
            if turn == 0:
                place, pace = position[:, at], velocity[:, at]
                heft = mass[pl.ds(block, 1), :]
            else:
                state = arrived(0, block)
                place, pace, heft = state[0:3], state[4:7], state[3:4]
            half[block, 0:3, :] = place + HALF * pace
            half[block, 3:4, :] = heft
            speed[block, 0:3, :] = pace
            return 0

        lax.fori_loop(0, blocks, load_block, 0, unroll=4)

        for distance in range(members):
            listed = ints[let_at + lax.rem(member + distance, members)]
            whole = half[listed]
            if distance == 0:
                let_in[turn, 0] = whole[0:4]
            else:
                let_out[turn, distance] = whole[0:4]
        if turn == 0:
            pl.semaphore_wait(barrier, members + groups - 2)
        for distance in range(1, members):
            let_copy(turn, distance).start()

        per_block = BLOCK // CELL
        offset = lax.rem(group, per_chunk) * publish
        found = jnp.zeros((ROWS, BLOCK), jnp.float32)
        for entry in range(publish):
            cell = ints[cells_at + entry]
            block = half[cell // per_block]
            heft = block[3:4]
            weighted = jnp.where(row < 3, block * heft, block)
            inside = lane // CELL == cell % per_block
            total = jnp.sum(jnp.where(inside, weighted, 0.0), axis=1, keepdims=True)
            found = jnp.where(lane == offset + entry, total, found)
        held = (lane >= offset) & (lane < offset + publish)
        heft = jnp.where(held, found[3:4], 1.0)
        found = jnp.where(row < 3, found / heft, found)
        if chunks > 1:
            cell_out[turn] = jnp.zeros_like(cell_out[turn])
        cell_out[turn, group // per_chunk] = found
        for distance in range(1, groups):
            cell_copy(turn, distance).start()

        def featurise(block, _):
            here = half[block]
            columns[block], moments[block] = source_features(here)
            targets[block] = target_features(here)
            return 0

        lax.fori_loop(0, blocks, featurise, 0, unroll=4)

        for distance in range(1, groups):
            cell_copy(turn, distance).wait_recv()
        for chunk in range(chunks):
            total = cell_in[turn, 1, chunk]
            for distance in range(2, groups):
                total = total + cell_in[turn, distance, chunk]
            far_columns[chunk], far_moments[chunk] = source_features(total)

        for distance in range(1, members):
            let_copy(turn, distance).wait_recv()

        def featurise_listed(distance, _):
            spread = jnp.concatenate(
                [let_in[turn, distance], jnp.zeros((4, BLOCK), jnp.float32)], axis=0
            )
            columns[blocks + distance], moments[blocks + distance] = source_features(spread)
            return 0

        lax.fori_loop(0, members, featurise_listed, 0, unroll=2)

        def chunk(step, _):
            reach = [distance_at(step * together + inner) for inner in range(together)]
            places = [(far_off, rank) for far_off in reach for rank in range(capacity)]
            at = order_at + turn * slots
            owned = [ints[at + far_off * capacity + rank] for far_off, rank in places]

            def spread(_, carry):
                for index, block in enumerate(owned):
                    near_columns = jnp.concatenate(
                        [columns[ints[block * entries + entry]] for entry in range(entries)]
                        + [far_columns[piece] for piece in range(chunks)],
                        axis=0,
                    )
                    weights[index] = weights_of(
                        jnp.dot(near_columns, targets[block], preferred_element_type=jnp.float32)
                    )
                return carry

            lax.fori_loop(0, once, spread, 0)

            def gather(_, carry):
                for index, block in enumerate(owned):
                    far_off, rank = places[index]
                    length = ints[lengths_at + block]
                    near_moments = jnp.concatenate(
                        [
                            moments[ints[block * entries + entry]]
                            * (entry < length).astype(jnp.float32).astype(jnp.bfloat16)
                            for entry in range(entries)
                        ]
                        + [far_moments[piece] for piece in range(chunks)],
                        axis=1,
                    )
                    sums = fold(
                        jnp.dot(near_moments, weights[index], preferred_element_type=jnp.float32)
                    )
                    here = half[block, 0:4]
                    pull = sums[0:3] - here[0:3] * sums[3:4]
                    pace = speed[block, 0:3] + TIMESTEP * pull
                    move_out[turn, far_off, rank, 0:3, :] = here[0:3] + HALF * pace
                    move_out[turn, far_off, rank, 3:4, :] = here[3:4]
                    move_out[turn, far_off, rank, 4:7, :] = pace
                return carry

            lax.fori_loop(0, once, gather, 0)

            for far_off in reach[:-1]:
                move_copy(turn, far_off).start()

            @pl.when(step < members // together - 1)
            def _():
                move_copy(turn, reach[-1]).start()

            return 0

        lax.fori_loop(0, members // together, chunk, 0)
        for rank in range(capacity):
            move_in[turn, 0, rank] = move_out[turn, 0, rank]
        for distance in range(1, members):
            move_copy(turn, distance).wait_recv()

    def unload(block, _):
        at = pl.ds(pl.multiple_of(block * BLOCK, BLOCK), BLOCK)
        state = arrived(1, block)
        out_position[:, at] = state[0:3]
        out_velocity[:, at] = state[4:7]
        out_mass[pl.ds(block, 1), :] = state[3:4]
        return 0

    lax.fori_loop(0, blocks, unload, 0, unroll=4)
    for turn in range(2):
        for distance in range(1, members):
            let_copy(turn, distance).wait_send()
            move_copy(turn, distance).wait_send()
        for distance in range(1, groups):
            cell_copy(turn, distance).wait_send()


def shards(position, velocity, mass, neighbours, list_length, let_list, cell_list, destination):
    members, groups = lax.axis_size("member"), lax.axis_size("group")
    member = lax.axis_index("member")
    blocks, entries = neighbours.shape
    publish = cell_list.shape[1]
    capacity = (blocks + members - 1) // members
    slots = members * capacity
    chunks = max(1, groups * publish // BLOCK)

    shift = (destination - member) % members
    number = jnp.arange(blocks, dtype=jnp.int32)
    same = (shift[:, :, None] == shift[:, None, :]) & (number[None, :] < number[:, None])
    slot = shift * capacity + jnp.sum(same, axis=2, dtype=jnp.int32)
    hit = slot[:, None, :] == jnp.arange(slots, dtype=jnp.int32)[None, :, None]
    order = jnp.sum(jnp.where(hit, number[None, None, :], 0), axis=2, dtype=jnp.int32)
    pool = jnp.where(
        neighbours < blocks, neighbours, blocks + (member - (neighbours - blocks)) % members
    )
    ints = jnp.concatenate(
        [
            pool.reshape(-1),
            list_length,
            let_list.reshape(-1),
            cell_list.reshape(-1),
            order.reshape(-1),
            slot.reshape(-1),
        ]
    )
    vmem = pl.BlockSpec(memory_space=pltpu.VMEM)
    f32, bf16 = jnp.float32, jnp.bfloat16
    pool_size = blocks + members
    dma = pltpu.SemaphoreType.DMA
    results = pl.pallas_call(
        functools.partial(kernel, (blocks, entries, members, groups, capacity, publish)),
        out_shape=(
            jax.ShapeDtypeStruct(position.shape, f32),
            jax.ShapeDtypeStruct(velocity.shape, f32),
            jax.ShapeDtypeStruct((blocks, BLOCK), f32),
        ),
        in_specs=[pl.BlockSpec(memory_space=pltpu.SMEM), vmem, vmem, vmem],
        out_specs=(vmem, vmem, vmem),
        scratch_shapes=[
            pltpu.VMEM((blocks, ROWS, BLOCK), f32),
            pltpu.VMEM((blocks, ROWS, BLOCK), f32),
            pltpu.VMEM((pool_size, BLOCK, FEATS), bf16),
            pltpu.VMEM((pool_size, 2 * ROWS, BLOCK), bf16),
            pltpu.VMEM((blocks, FEATS, BLOCK), bf16),
            pltpu.VMEM((max(GATHERED, capacity), (entries + chunks) * BLOCK, BLOCK), bf16),
            pltpu.VMEM((chunks, BLOCK, FEATS), bf16),
            pltpu.VMEM((chunks, 2 * ROWS, BLOCK), bf16),
            pltpu.VMEM((2, members, 4, BLOCK), f32),
            pltpu.VMEM((2, members, 4, BLOCK), f32),
            pltpu.VMEM((2, chunks, ROWS, BLOCK), f32),
            pltpu.VMEM((2, groups, chunks, ROWS, BLOCK), f32),
            pltpu.VMEM((2, members, capacity, 7, BLOCK), f32),
            pltpu.VMEM((2, members, capacity, 7, BLOCK), f32),
            dma((2, members)),
            dma((2, members)),
            dma((2, groups)),
            dma((2, groups)),
            dma((2, members)),
            dma((2, members)),
        ],
        compiler_params=pltpu.CompilerParams(
            collective_id=0, has_side_effects=True, vmem_limit_bytes=48 * 1024 * 1024
        ),
        name="two_steps",
    )(ints, position, velocity, mass.reshape(blocks, BLOCK))
    return results[0], results[1], results[2].reshape(-1)


def solution(mesh):
    shared = ("group", "member")
    return jax.shard_map(
        shards,
        mesh=mesh,
        in_specs=(
            P(None, shared),
            P(None, shared),
            P(shared),
            P(shared, None),
            P(shared),
            P(shared, None),
            P(shared, None),
            P(None, shared),
        ),
        out_specs=(P(None, shared), P(None, shared), P(shared)),
        check_vma=False,
    )
```

```python
import functools

import jax
import jax.numpy as jnp
from jax import lax
from jax.experimental import pallas as pl
from jax.experimental.pallas import tpu as pltpu
from jax.sharding import PartitionSpec as P

BLOCK = 128
CELL = 16
SOFTENING = 0.01
TIMESTEP = 0.1
ROWS = 8
FEATS = 64
HALF = 0.5 * TIMESTEP
GATHERED = 16


def parts_of(value):
    high = value.astype(jnp.bfloat16).astype(jnp.float32)
    rest = value - high
    middle = rest.astype(jnp.bfloat16).astype(jnp.float32)
    return high, middle, rest - middle


def rows_of(shape):
    return lax.broadcasted_iota(jnp.int32, shape, 0)


def source_features(block):
    row = rows_of(block.shape)
    mass = block[3:4]
    square = jnp.sum(jnp.where(row < 3, block * block, 0.0), axis=0, keepdims=True)
    tail = jnp.where(row == 3, square, jnp.where(row == 4, 1.0, 0.0))
    high, middle, low = parts_of(jnp.where(row < 3, block, tail))
    columns = jnp.concatenate([high, high, high, middle, middle, middle, low, low], axis=0)
    weighted = jnp.where(row < 3, block * mass, jnp.where(row == 3, mass, 0.0))
    heavy, light, least = [part[0:4] for part in parts_of(weighted)]
    moments = jnp.concatenate([heavy, light, least, jnp.zeros_like(least)], axis=0)
    return jnp.transpose(columns).astype(jnp.bfloat16), moments.astype(jnp.bfloat16)


def target_features(block):
    row = rows_of(block.shape)
    square = jnp.sum(jnp.where(row < 3, block * block, 0.0), axis=0, keepdims=True)
    tail = jnp.where(row == 3, 1.0, jnp.where(row == 4, square + SOFTENING, 0.0))
    high, middle, low = parts_of(jnp.where(row < 3, -2.0 * block, tail))
    rows = jnp.concatenate([high, middle, low, high, middle, low, high, middle], axis=0)
    return rows.astype(jnp.bfloat16)


def weights_of(radius_sq):
    inverse = lax.rsqrt(radius_sq)
    return (inverse * inverse * inverse).astype(jnp.bfloat16)


def fold(sums):
    pair = sums[0:8] + sums[8:16]
    return pair[0:4] + pair[4:8]


def migration(destination, member, members, blocks, capacity):
    lane = lax.broadcasted_iota(jnp.int32, (1, BLOCK), 1)
    spare = jnp.zeros((1, BLOCK - blocks), jnp.int32)
    shift = jnp.concatenate([destination, spare], axis=1) - member
    shift = jnp.where(shift < 0, shift + members, shift)
    shift = jnp.where(lane < blocks, shift, members)
    rows = -(-members // ROWS) * ROWS
    row = rows_of((rows, BLOCK))
    lanes = lax.broadcasted_iota(jnp.int32, (rows, BLOCK), 1)
    mine = jnp.where(row == shift, 1, 0)
    count, step = mine, 1
    while step < blocks:
        count = count + jnp.where(lanes >= step, pltpu.roll(count, step, 1), 0)
        step *= 2
    rank = jnp.sum(mine * (count - 1), axis=0, keepdims=True)
    slot = jnp.where(lane < blocks, shift * capacity + rank, -1)
    across = jnp.transpose(jnp.broadcast_to(slot, (BLOCK, BLOCK)))
    square = lax.broadcasted_iota(jnp.int32, (BLOCK, BLOCK), 1)
    order = jnp.sum(jnp.where(across == square, rows_of((BLOCK, BLOCK)), 0), axis=0, keepdims=True)
    return order, jnp.clip(slot, 0, members * capacity - 1)


def kernel(
    sizes,
    position_hbm,
    velocity_hbm,
    mass_hbm,
    neighbours_hbm,
    length_hbm,
    let_hbm,
    cell_hbm,
    destination_hbm,
    out_position,
    out_velocity,
    out_mass,
    position,
    velocity,
    mass,
    neighbours,
    lengths,
    lets,
    cells,
    destination,
    tables,
    table,
    half,
    speed,
    columns,
    moments,
    targets,
    weights,
    far_columns,
    far_moments,
    let_out,
    let_in,
    cell_out,
    cell_in,
    early_out,
    early_first,
    early_second,
    late_out,
    late_in,
    load_sem,
    let_send,
    let_recv,
    cell_send,
    cell_recv,
    early_send,
    early_recv,
    late_send,
    late_recv,
):
    blocks, entries, members, groups, capacity, publish = sizes
    slots = members * capacity
    chunks = far_columns.shape[0]
    per_chunk = groups // chunks
    group, member = lax.axis_index("group"), lax.axis_index("member")
    early_in = (early_first, early_second)

    loads = [
        pltpu.make_async_copy(one, other, load_sem.at[at])
        for at, (one, other) in enumerate(
            (
                (destination_hbm, destination),
                (position_hbm, position),
                (velocity_hbm, velocity),
                (mass_hbm, mass),
                (let_hbm, lets),
                (cell_hbm, cells),
                (neighbours_hbm, neighbours),
                (length_hbm, lengths),
                (tables, table),
            )
        )
    ]
    for load in loads[:-1]:
        load.start()

    def peer(distance):
        return {"member": lax.rem(member + distance, members)}

    def group_peer(distance):
        return {"group": lax.rem(group + distance, groups)}

    mesh_id = pl.DeviceIdType.MESH
    barrier = pltpu.get_barrier_semaphore()
    for distance in range(1, members):
        pl.semaphore_signal(barrier, inc=1, device_id=peer(distance), device_id_type=mesh_id)
    for distance in range(1, groups):
        pl.semaphore_signal(barrier, inc=1, device_id=group_peer(distance), device_id_type=mesh_id)

    def let_copy(turn, distance):
        return pltpu.make_async_remote_copy(
            src_ref=let_out.at[turn, distance],
            dst_ref=let_in.at[turn, distance],
            send_sem=let_send.at[turn, distance],
            recv_sem=let_recv.at[turn, distance],
            device_id=peer(distance),
            device_id_type=mesh_id,
        )

    def cell_copy(turn, distance):
        return pltpu.make_async_remote_copy(
            src_ref=cell_out.at[turn],
            dst_ref=cell_in.at[turn, distance],
            send_sem=cell_send.at[turn, distance],
            recv_sem=cell_recv.at[turn, distance],
            device_id=group_peer(distance),
            device_id_type=mesh_id,
        )

    def early_copy(turn, distance):
        return pltpu.make_async_remote_copy(
            src_ref=early_out.at[turn, distance],
            dst_ref=early_in[turn].at[distance],
            send_sem=early_send.at[turn, distance],
            recv_sem=early_recv.at[turn, distance],
            device_id=peer(distance),
            device_id_type=mesh_id,
        )

    def late_copy(turn, distance):
        return pltpu.make_async_remote_copy(
            src_ref=late_out.at[turn, distance],
            dst_ref=late_in.at[turn, distance],
            send_sem=late_send.at[turn, distance],
            recv_sem=late_recv.at[turn, distance],
            device_id=peer(distance),
            device_id_type=mesh_id,
        )

    def arrived(turn, block):
        slot = table[2 * turn + 1, block]
        far_off, rank = slot // capacity, slot % capacity
        before, pace = early_in[turn][far_off, rank], late_in[turn, far_off, rank]
        return before[0:3] + HALF * pace, pace, before[3:4]

    def source(block, entry):
        return jnp.where(entry < lengths[block], neighbours[entry, block], blocks + members)

    together = max(1, min(members, GATHERED // capacity))
    while members % together:
        together -= 1
    once = jnp.minimum(member + 1, 1)

    def distance_at(index):
        swing = (index + 1) // 2
        away = members // 2 + jnp.where(index % 2 == 1, -swing, swing)
        return jnp.where(index == members - 1, 0, away)

    speed[...] = jnp.zeros_like(speed)
    half[...] = jnp.zeros_like(half)
    columns[blocks + members], moments[blocks + members] = source_features(
        jnp.zeros((ROWS, BLOCK), jnp.float32)
    )
    row = rows_of((ROWS, BLOCK))
    lane = lax.broadcasted_iota(jnp.int32, (ROWS, BLOCK), 1)

    loads[0].wait()
    for turn in range(2):
        order, slot = migration(destination[turn : turn + 1, :], member, members, blocks, capacity)
        tables[2 * turn : 2 * turn + 1, :] = order
        tables[2 * turn + 1 : 2 * turn + 2, :] = slot
    loads[-1].start()
    for load in loads[1:4]:
        load.wait()

    for turn in range(2):

        def load_block(block, _):
            at = pl.ds(pl.multiple_of(block * BLOCK, BLOCK), BLOCK)
            if turn == 0:
                place, pace = position[:, at], velocity[:, at]
                heft = mass[pl.ds(block, 1), :]
            else:
                place, pace, heft = arrived(0, block)
            half[block, 0:3, :] = place + HALF * pace
            half[block, 3:4, :] = heft
            speed[block, 0:3, :] = pace
            return 0

        lax.fori_loop(0, blocks, load_block, 0, unroll=4)

        if turn == 0:
            for load in loads[4:8]:
                load.wait()
        for distance in range(members):
            listed = lets[0, lax.rem(member + distance, members)]
            whole = half[listed]
            if distance == 0:
                let_in[turn, 0] = whole[0:4]
            else:
                let_out[turn, distance] = whole[0:4]
        if turn == 0:
            pl.semaphore_wait(barrier, members + groups - 2)
        for distance in range(1, members):
            let_copy(turn, distance).start()

        per_block = BLOCK // CELL
        offset = lax.rem(group, per_chunk) * publish
        found = jnp.zeros((ROWS, BLOCK), jnp.float32)
        for entry in range(publish):
            cell = cells[0, entry]
            block = half[cell // per_block]
            heft = block[3:4]
            weighted = jnp.where(row < 3, block * heft, block)
            inside = lane // CELL == cell % per_block
            total = jnp.sum(jnp.where(inside, weighted, 0.0), axis=1, keepdims=True)
            found = jnp.where(lane == offset + entry, total, found)
        held = (lane >= offset) & (lane < offset + publish)
        heft = jnp.where(held, found[3:4], 1.0)
        found = jnp.where(row < 3, found / heft, found)
        if chunks > 1:
            cell_out[turn] = jnp.zeros_like(cell_out[turn])
        cell_out[turn, group // per_chunk] = found
        for distance in range(1, groups):
            cell_copy(turn, distance).start()

        if turn == 0:
            loads[-1].wait()
        for distance in range(1, members):
            for rank in range(capacity):
                early_out[turn, distance, rank] = half[table[2 * turn, distance * capacity + rank], 0:4]
            early_copy(turn, distance).start()
        for rank in range(capacity):
            early_in[turn][0, rank] = half[table[2 * turn, rank], 0:4]

        def featurise(block, _):
            here = half[block]
            columns[block], moments[block] = source_features(here)
            targets[block] = target_features(here)
            return 0

        lax.fori_loop(0, blocks, featurise, 0, unroll=4)

        for distance in range(1, groups):
            cell_copy(turn, distance).wait_recv()
        for chunk in range(chunks):
            total = cell_in[turn, 1, chunk]
            for distance in range(2, groups):
                total = total + cell_in[turn, distance, chunk]
            far_columns[chunk], far_moments[chunk] = source_features(total)

        for distance in range(1, members):
            let_copy(turn, distance).wait_recv()

        def featurise_listed(distance, _):
            spread = jnp.concatenate(
                [let_in[turn, distance], jnp.zeros((4, BLOCK), jnp.float32)], axis=0
            )
            at = blocks + lax.rem(member + members - distance, members)
            columns[at], moments[at] = source_features(spread)
            return 0

        lax.fori_loop(0, members, featurise_listed, 0, unroll=2)

        def chunk(step, _):
            reach = [distance_at(step * together + inner) for inner in range(together)]
            places = [(far_off, rank) for far_off in reach for rank in range(capacity)]
            owned = [table[2 * turn, far_off * capacity + rank] for far_off, rank in places]

            def spread(_, carry):
                for index, block in enumerate(owned):
                    near_columns = jnp.concatenate(
                        [columns[source(block, entry)] for entry in range(entries)]
                        + [far_columns[piece] for piece in range(chunks)],
                        axis=0,
                    )
                    weights[index] = weights_of(
                        jnp.dot(near_columns, targets[block], preferred_element_type=jnp.float32)
                    )
                return carry

            lax.fori_loop(0, once, spread, 0)

            def gather(_, carry):
                for index, block in enumerate(owned):
                    far_off, rank = places[index]
                    near_moments = jnp.concatenate(
                        [moments[source(block, entry)] for entry in range(entries)]
                        + [far_moments[piece] for piece in range(chunks)],
                        axis=1,
                    )
                    sums = fold(
                        jnp.dot(near_moments, weights[index], preferred_element_type=jnp.float32)
                    )
                    here = half[block, 0:4]
                    pull = sums[0:3] - here[0:3] * sums[3:4]
                    pace = speed[block, 0:3] + TIMESTEP * pull
                    late_out[turn, far_off, rank] = pace
                return carry

            lax.fori_loop(0, once, gather, 0)

            for far_off in reach[:-1]:
                late_copy(turn, far_off).start()

            @pl.when(step < members // together - 1)
            def _():
                late_copy(turn, reach[-1]).start()

            return 0

        lax.fori_loop(0, members // together, chunk, 0)
        for rank in range(capacity):
            late_in[turn, 0, rank] = late_out[turn, 0, rank]
        for distance in range(1, members):
            early_copy(turn, distance).wait_recv()
            late_copy(turn, distance).wait_recv()

    def unload(block, _):
        at = pl.ds(pl.multiple_of(block * BLOCK, BLOCK), BLOCK)
        out_position[:, at], out_velocity[:, at], out_mass[pl.ds(block, 1), :] = arrived(1, block)
        return 0

    lax.fori_loop(0, blocks, unload, 0, unroll=4)
    for turn in range(2):
        for distance in range(1, members):
            let_copy(turn, distance).wait_send()
            early_copy(turn, distance).wait_send()
            late_copy(turn, distance).wait_send()
        for distance in range(1, groups):
            cell_copy(turn, distance).wait_send()


def put_out(position, velocity, mass, final_position, final_velocity, final_mass, sent):
    pairs = ((position, final_position), (velocity, final_velocity), (mass, final_mass))
    copies = [pltpu.make_async_copy(one, other, sent.at[at]) for at, (one, other) in enumerate(pairs)]
    for copy in copies:
        copy.start()
    for copy in copies:
        copy.wait()


def shards(position, velocity, mass, neighbours, list_length, let_list, cell_list, destination):
    members, groups = lax.axis_size("member"), lax.axis_size("group")
    member = lax.axis_index("member")
    blocks, entries = neighbours.shape
    publish = cell_list.shape[1]
    capacity = (blocks + members - 1) // members
    chunks = max(1, groups * publish // BLOCK)
    vmem = pl.BlockSpec(memory_space=pltpu.VMEM)
    f32, bf16 = jnp.float32, jnp.bfloat16
    pool_size = blocks + members + 1
    dma = pltpu.SemaphoreType.DMA
    results = pl.pallas_call(
        functools.partial(kernel, (blocks, entries, members, groups, capacity, publish)),
        out_shape=(
            jax.ShapeDtypeStruct(position.shape, f32),
            jax.ShapeDtypeStruct(velocity.shape, f32),
            jax.ShapeDtypeStruct((blocks, BLOCK), f32),
        ),
        in_specs=[pl.BlockSpec(memory_space=pltpu.HBM)] * 8,
        out_specs=(vmem, vmem, vmem),
        scratch_shapes=[
            pltpu.VMEM(position.shape, f32),
            pltpu.VMEM(velocity.shape, f32),
            pltpu.VMEM((blocks, BLOCK), f32),
            pltpu.SMEM((entries, blocks), jnp.int32),
            pltpu.SMEM(list_length.shape, jnp.int32),
            pltpu.SMEM(let_list.shape, jnp.int32),
            pltpu.SMEM(cell_list.shape, jnp.int32),
            pltpu.VMEM(destination.shape, jnp.int32),
            pltpu.VMEM((4, BLOCK), jnp.int32),
            pltpu.SMEM((4, BLOCK), jnp.int32),
            pltpu.VMEM((blocks, ROWS, BLOCK), f32),
            pltpu.VMEM((blocks, ROWS, BLOCK), f32),
            pltpu.VMEM((pool_size, BLOCK, FEATS), bf16),
            pltpu.VMEM((pool_size, 2 * ROWS, BLOCK), bf16),
            pltpu.VMEM((blocks, FEATS, BLOCK), bf16),
            pltpu.VMEM((max(GATHERED, capacity), (entries + chunks) * BLOCK, BLOCK), bf16),
            pltpu.VMEM((chunks, BLOCK, FEATS), bf16),
            pltpu.VMEM((chunks, 2 * ROWS, BLOCK), bf16),
            pltpu.VMEM((2, members, 4, BLOCK), f32),
            pltpu.VMEM((2, members, 4, BLOCK), f32),
            pltpu.VMEM((2, chunks, ROWS, BLOCK), f32),
            pltpu.VMEM((2, groups, chunks, ROWS, BLOCK), f32),
            pltpu.VMEM((2, members, capacity, 4, BLOCK), f32),
            pltpu.VMEM((members, capacity, 4, BLOCK), f32),
            pltpu.VMEM((members, capacity, 4, BLOCK), f32),
            pltpu.VMEM((2, members, capacity, 3, BLOCK), f32),
            pltpu.VMEM((2, members, capacity, 3, BLOCK), f32),
            dma((9,)),
            dma((2, members)),
            dma((2, members)),
            dma((2, groups)),
            dma((2, groups)),
            dma((2, members)),
            dma((2, members)),
            dma((2, members)),
            dma((2, members)),
        ],
        compiler_params=pltpu.CompilerParams(
            collective_id=0, has_side_effects=True, vmem_limit_bytes=40 * 1024 * 1024
        ),
        name="two_steps",
    )(
        *(
            pltpu.with_memory_space_constraint(array, pltpu.HBM)
            for array in (
                position,
                velocity,
                mass.reshape(blocks, BLOCK),
                neighbours.T,
                list_length,
                let_list,
                cell_list,
                destination,
            )
        )
    )
    whole = pl.BlockSpec(memory_space=pl.ANY)
    return pl.pallas_call(
        put_out,
        out_shape=(
            jax.ShapeDtypeStruct(position.shape, f32),
            jax.ShapeDtypeStruct(velocity.shape, f32),
            jax.ShapeDtypeStruct(mass.shape, f32),
        ),
        in_specs=[vmem] * 3,
        out_specs=(whole,) * 3,
        scratch_shapes=[dma((3,))],
        compiler_params=pltpu.CompilerParams(vmem_limit_bytes=2 * 1024 * 1024),
        name="put_out",
    )(results[0], results[1], results[2].reshape(-1))


def solution(mesh):
    shared = ("group", "member")
    return jax.shard_map(
        shards,
        mesh=mesh,
        in_specs=(
            P(None, shared),
            P(None, shared),
            P(shared),
            P(shared, None),
            P(shared),
            P(shared, None),
            P(shared, None),
            P(None, shared),
        ),
        out_specs=(P(None, shared), P(None, shared), P(shared)),
        check_vma=False,
    )
```

```python
import functools
import math

import jax
import jax.numpy as jnp
from jax import lax
from jax.experimental import pallas as pl
from jax.experimental.pallas import tpu as pltpu
from jax.sharding import PartitionSpec as P

BLOCK = 128
CELL = 16
SOFTENING = 0.01
TIMESTEP = 0.1
ROWS = 8
FEATS = 64
HALF = 0.5 * TIMESTEP
GATHERED = 16


def parts_of(value):
    high = value.astype(jnp.bfloat16).astype(jnp.float32)
    rest = value - high
    middle = rest.astype(jnp.bfloat16).astype(jnp.float32)
    return high, middle, rest - middle


def rows_of(shape):
    return lax.broadcasted_iota(jnp.int32, shape, 0)


def source_features(block):
    row = rows_of(block.shape)
    mass = block[3:4]
    square = jnp.sum(jnp.where(row < 3, block * block, 0.0), axis=0, keepdims=True)
    tail = jnp.where(row == 3, square, jnp.where(row == 4, 1.0, 0.0))
    high, middle, low = parts_of(jnp.where(row < 3, block, tail))
    columns = jnp.concatenate([high, high, high, middle, middle, middle, low, low], axis=0)
    weighted = jnp.where(row < 3, block * mass, jnp.where(row == 3, mass, 0.0))
    heavy, light, least = [part[0:4] for part in parts_of(weighted)]
    moments = jnp.concatenate([heavy, light, least, jnp.zeros_like(least)], axis=0)
    return jnp.transpose(columns).astype(jnp.bfloat16), moments.astype(jnp.bfloat16)


def target_features(block):
    row = rows_of(block.shape)
    square = jnp.sum(jnp.where(row < 3, block * block, 0.0), axis=0, keepdims=True)
    tail = jnp.where(row == 3, 1.0, jnp.where(row == 4, square + SOFTENING, 0.0))
    high, middle, low = parts_of(jnp.where(row < 3, -2.0 * block, tail))
    rows = jnp.concatenate([high, middle, low, high, middle, low, high, middle], axis=0)
    return rows.astype(jnp.bfloat16)


def weights_of(radius_sq):
    inverse = lax.rsqrt(radius_sq)
    return (inverse * inverse * inverse).astype(jnp.bfloat16)


def fold(sums):
    pair = sums[0:8] + sums[8:16]
    return pair[0:4] + pair[4:8]


def migration(destination, member, members, blocks, capacity):
    lane = lax.broadcasted_iota(jnp.int32, (1, BLOCK), 1)
    spare = jnp.zeros((1, BLOCK - blocks), jnp.int32)
    shift = jnp.concatenate([destination, spare], axis=1) - member
    shift = jnp.where(shift < 0, shift + members, shift)
    shift = jnp.where(lane < blocks, shift, members)
    rows = -(-members // ROWS) * ROWS
    row = rows_of((rows, BLOCK))
    lanes = lax.broadcasted_iota(jnp.int32, (rows, BLOCK), 1)
    mine = jnp.where(row == shift, 1, 0)
    count, step = mine, 1
    while step < blocks:
        count = count + jnp.where(lanes >= step, pltpu.roll(count, step, 1), 0)
        step *= 2
    rank = jnp.sum(mine * (count - 1), axis=0, keepdims=True)
    slot = jnp.where(lane < blocks, shift * capacity + rank, -1)
    across = jnp.transpose(jnp.broadcast_to(slot, (BLOCK, BLOCK)))
    square = lax.broadcasted_iota(jnp.int32, (BLOCK, BLOCK), 1)
    order = jnp.sum(jnp.where(across == square, rows_of((BLOCK, BLOCK)), 0), axis=0, keepdims=True)
    return order, jnp.clip(slot, 0, members * capacity - 1)


def kernel(
    sizes,
    position_hbm,
    velocity_hbm,
    mass_hbm,
    neighbours_hbm,
    length_hbm,
    let_hbm,
    cell_hbm,
    destination_hbm,
    out_position,
    out_velocity,
    out_mass,
    position,
    velocity,
    mass,
    neighbours,
    lengths,
    lets,
    cells,
    destination,
    tables,
    table,
    half,
    speed,
    columns,
    moments,
    targets,
    first_weights,
    second_weights,
    far_weights,
    far_columns,
    far_moments,
    let_out,
    let_in,
    cell_out,
    cell_in,
    early_out,
    early_first,
    early_second,
    late_out,
    late_first,
    late_second,
    load_sem,
    let_send,
    let_recv,
    cell_send,
    cell_recv,
    early_send,
    early_recv,
    late_send,
    late_recv,
):
    blocks, entries, members, groups, capacity, publish = sizes
    slots = members * capacity
    chunks = far_columns.shape[0]
    per_chunk = groups // chunks
    group, member = lax.axis_index("group"), lax.axis_index("member")
    early_in, late_in = (early_first, early_second), (late_first, late_second)
    weights = (first_weights, second_weights)

    loads = [
        pltpu.make_async_copy(one, other, load_sem.at[at])
        for at, (one, other) in enumerate(
            (
                (destination_hbm, destination),
                (position_hbm, position),
                (velocity_hbm, velocity),
                (mass_hbm, mass),
                (let_hbm, lets),
                (cell_hbm, cells),
                (neighbours_hbm, neighbours),
                (length_hbm, lengths),
                (tables, table),
            )
        )
    ]
    for load in loads[:-1]:
        load.start()

    def peer(distance):
        return {"member": lax.rem(member + distance, members)}

    def group_peer(distance):
        return {"group": lax.rem(group + distance, groups)}

    mesh_id = pl.DeviceIdType.MESH
    barrier = pltpu.get_barrier_semaphore()
    for distance in range(1, members):
        pl.semaphore_signal(barrier, inc=1, device_id=peer(distance), device_id_type=mesh_id)
    for distance in range(1, groups):
        pl.semaphore_signal(barrier, inc=1, device_id=group_peer(distance), device_id_type=mesh_id)

    def let_copy(turn, distance):
        return pltpu.make_async_remote_copy(
            src_ref=let_out.at[turn, distance],
            dst_ref=let_in.at[turn, distance],
            send_sem=let_send.at[turn, distance],
            recv_sem=let_recv.at[turn, distance],
            device_id=peer(distance),
            device_id_type=mesh_id,
        )

    def cell_copy(turn, distance):
        return pltpu.make_async_remote_copy(
            src_ref=cell_out.at[turn],
            dst_ref=cell_in.at[turn, distance],
            send_sem=cell_send.at[turn, distance],
            recv_sem=cell_recv.at[turn, distance],
            device_id=group_peer(distance),
            device_id_type=mesh_id,
        )

    def early_copy(turn, distance):
        return pltpu.make_async_remote_copy(
            src_ref=early_out.at[turn, distance],
            dst_ref=early_in[turn].at[distance],
            send_sem=early_send.at[turn, distance],
            recv_sem=early_recv.at[turn, distance],
            device_id=peer(distance),
            device_id_type=mesh_id,
        )

    def late_copy(turn, distance):
        return pltpu.make_async_remote_copy(
            src_ref=late_out.at[turn, distance],
            dst_ref=late_in[turn].at[distance],
            send_sem=late_send.at[turn, distance],
            recv_sem=late_recv.at[turn, distance],
            device_id=peer(distance),
            device_id_type=mesh_id,
        )

    def arrived(turn, block):
        slot = table[2 * turn + 1, block]
        far_off, rank = slot // capacity, slot % capacity
        before, pace = early_in[turn][far_off, rank], late_in[turn][far_off, rank]
        return before[0:3] + HALF * pace, pace, before[3:4]

    def source(block, entry):
        return jnp.where(entry < lengths[block], neighbours[entry, block], blocks + members)

    route = [*range(1, members - 2), *range(members - 1, members - 3, -1)]
    together = max(1, GATHERED // capacity)
    parties = [route[first : first + together] for first in range(0, len(route), together)] + [[0]]

    speed[...] = jnp.zeros_like(speed)
    half[...] = jnp.zeros_like(half)
    columns[blocks + members], moments[blocks + members] = source_features(
        jnp.zeros((ROWS, BLOCK), jnp.float32)
    )
    row = rows_of((ROWS, BLOCK))
    lane = lax.broadcasted_iota(jnp.int32, (ROWS, BLOCK), 1)

    loads[0].wait()
    for turn in range(2):
        order, slot = migration(destination[turn : turn + 1, :], member, members, blocks, capacity)
        tables[2 * turn : 2 * turn + 1, :] = order
        tables[2 * turn + 1 : 2 * turn + 2, :] = slot
    loads[-1].start()
    for load in loads[1:-1]:
        load.wait()

    for turn in range(2):

        def load_block(block, _):
            if turn == 0:
                at = pl.ds(pl.multiple_of(block * BLOCK, BLOCK), BLOCK)
                place, pace, heft = position[:, at], velocity[:, at], mass[pl.ds(block, 1), :]
            else:
                place, pace, heft = arrived(0, block)
            half[block, 0:3, :] = place + HALF * pace
            half[block, 3:4, :] = heft
            speed[block, 0:3, :] = pace
            return 0

        if turn == 0:
            lax.fori_loop(0, blocks, load_block, 0, unroll=4)
        for distance in range(members):
            listed = lets[0, lax.rem(member + distance, members)]
            into = let_out if distance else let_in
            if turn == 0:
                into[turn, distance] = half[listed, 0:4]
            else:
                place, pace, heft = arrived(0, listed)
                into[turn, distance, 0:3, :] = place + HALF * pace
                into[turn, distance, 3:4, :] = heft
        if turn == 0:
            pl.semaphore_wait(barrier, members + groups - 2)
        for distance in route:
            let_copy(turn, distance).start()
        if turn == 1:
            lax.fori_loop(0, blocks, load_block, 0, unroll=4)

        per_block = BLOCK // CELL
        offset = lax.rem(group, per_chunk) * publish
        found = jnp.zeros((ROWS, BLOCK), jnp.float32)
        for entry in range(publish):
            cell = cells[0, entry]
            block = half[cell // per_block]
            heft = block[3:4]
            weighted = jnp.where(row < 3, block * heft, block)
            inside = lane // CELL == cell % per_block
            total = jnp.sum(jnp.where(inside, weighted, 0.0), axis=1, keepdims=True)
            found = jnp.where(lane == offset + entry, total, found)
        held = (lane >= offset) & (lane < offset + publish)
        heft = jnp.where(held, found[3:4], 1.0)
        found = jnp.where(row < 3, found / heft, found)
        if chunks > 1:
            cell_out[turn] = jnp.zeros_like(cell_out[turn])
        cell_out[turn, group // per_chunk] = found
        for distance in range(1, groups):
            cell_copy(turn, distance).start()

        if turn == 0:
            loads[-1].wait()
        for distance in route:
            for rank in range(capacity):
                early_out[turn, distance, rank] = half[table[2 * turn, distance * capacity + rank], 0:4]
            early_copy(turn, distance).start()
        for rank in range(capacity):
            early_in[turn][0, rank] = half[table[2 * turn, rank], 0:4]

        def featurise(block, _):
            here = half[block]
            columns[block], moments[block] = source_features(here)
            targets[block] = target_features(here)
            return 0

        lax.fori_loop(0, blocks, featurise, 0, unroll=4)

        for distance in range(1, groups):
            cell_copy(turn, distance).wait_recv()
        for chunk in range(chunks):
            total = cell_in[turn, 1, chunk]
            for distance in range(2, groups):
                total = total + cell_in[turn, distance, chunk]
            far_columns[chunk], far_moments[chunk] = source_features(total)

        wide = math.gcd(blocks, 2 * GATHERED)

        def spread_far(step, _):
            far_rows = jnp.concatenate([far_columns[piece] for piece in range(chunks)], axis=0)
            for inner in range(wide):
                block = step * wide + inner
                far_weights[block] = weights_of(
                    jnp.dot(far_rows, targets[block], preferred_element_type=jnp.float32)
                )
            return 0

        lax.fori_loop(0, blocks // wide, spread_far, 0)

        for distance in range(1, members):
            let_copy(turn, distance).wait_recv()

        def featurise_listed(distance, _):
            spread = jnp.concatenate(
                [let_in[turn, distance], jnp.zeros((4, BLOCK), jnp.float32)], axis=0
            )
            at = blocks + lax.rem(member + members - distance, members)
            columns[at], moments[at] = source_features(spread)
            return 0

        lax.fori_loop(0, members, featurise_listed, 0, unroll=2)

        def owned(party):
            return [
                (away, rank, table[2 * turn, away * capacity + rank])
                for away in party
                for rank in range(capacity)
            ]

        def spread(party, into):
            for index, (_, _, block) in enumerate(owned(party)):
                near_columns = jnp.concatenate(
                    [columns[source(block, entry)] for entry in range(entries)], axis=0
                )
                into[index] = weights_of(
                    jnp.dot(near_columns, targets[block], preferred_element_type=jnp.float32)
                )

        def gather(party, held):
            for index, (away, rank, block) in enumerate(owned(party)):
                all_moments = jnp.concatenate(
                    [moments[source(block, entry)] for entry in range(entries)]
                    + [far_moments[piece] for piece in range(chunks)],
                    axis=1,
                )
                all_weights = jnp.concatenate([held[index], far_weights[block]], axis=0)
                sums = fold(jnp.dot(all_moments, all_weights, preferred_element_type=jnp.float32))
                here = half[block, 0:3]
                pull = sums[0:3] - here * sums[3:4]
                into = late_out.at[turn] if away else late_in[turn]
                into[away, rank] = speed[block, 0:3] + TIMESTEP * pull

        def both(ahead, behind, parity):
            spread(ahead, weights[1 - parity])
            gather(behind, weights[parity])

        spread(parties[0], weights[0])
        for at, party in enumerate(parties[:-2]):
            both(parties[at + 1], party, at % 2)
            for away in party:
                late_copy(turn, away).start()
        held = weights[(len(parties) - 2) % 2]
        gather(parties[-2], held)
        for away in parties[-2]:
            late_copy(turn, away).start()
        spread(parties[-1], held)
        gather(parties[-1], held)
        for distance in range(1, members):
            early_copy(turn, distance).wait_recv()
            late_copy(turn, distance).wait_recv()

    def unload(block, _):
        at = pl.ds(pl.multiple_of(block * BLOCK, BLOCK), BLOCK)
        out_position[:, at], out_velocity[:, at], out_mass[pl.ds(block, 1), :] = arrived(1, block)
        return 0

    lax.fori_loop(0, blocks, unload, 0, unroll=4)
    for turn in range(2):
        for distance in range(1, members):
            let_copy(turn, distance).wait_send()
            early_copy(turn, distance).wait_send()
            late_copy(turn, distance).wait_send()
        for distance in range(1, groups):
            cell_copy(turn, distance).wait_send()


def put_out(position, velocity, mass, final_position, final_velocity, final_mass, sent):
    pairs = ((position, final_position), (velocity, final_velocity), (mass, final_mass))
    copies = [pltpu.make_async_copy(one, other, sent.at[at]) for at, (one, other) in enumerate(pairs)]
    for copy in copies:
        copy.start()
    for copy in copies:
        copy.wait()


def shards(position, velocity, mass, neighbours, list_length, let_list, cell_list, destination):
    members, groups = lax.axis_size("member"), lax.axis_size("group")
    member = lax.axis_index("member")
    blocks, entries = neighbours.shape
    publish = cell_list.shape[1]
    capacity = (blocks + members - 1) // members
    chunks = max(1, groups * publish // BLOCK)
    vmem = pl.BlockSpec(memory_space=pltpu.VMEM)
    f32, bf16 = jnp.float32, jnp.bfloat16
    pool_size = blocks + members + 1
    dma = pltpu.SemaphoreType.DMA
    results = pl.pallas_call(
        functools.partial(kernel, (blocks, entries, members, groups, capacity, publish)),
        out_shape=(
            jax.ShapeDtypeStruct(position.shape, f32),
            jax.ShapeDtypeStruct(velocity.shape, f32),
            jax.ShapeDtypeStruct((blocks, BLOCK), f32),
        ),
        in_specs=[pl.BlockSpec(memory_space=pltpu.HBM)] * 8,
        out_specs=(vmem, vmem, vmem),
        scratch_shapes=[
            pltpu.VMEM(position.shape, f32),
            pltpu.VMEM(velocity.shape, f32),
            pltpu.VMEM((blocks, BLOCK), f32),
            pltpu.SMEM((entries, blocks), jnp.int32),
            pltpu.SMEM(list_length.shape, jnp.int32),
            pltpu.SMEM(let_list.shape, jnp.int32),
            pltpu.SMEM(cell_list.shape, jnp.int32),
            pltpu.VMEM(destination.shape, jnp.int32),
            pltpu.VMEM((4, BLOCK), jnp.int32),
            pltpu.SMEM((4, BLOCK), jnp.int32),
            pltpu.VMEM((blocks, ROWS, BLOCK), f32),
            pltpu.VMEM((blocks, ROWS, BLOCK), f32),
            pltpu.VMEM((pool_size, BLOCK, FEATS), bf16),
            pltpu.VMEM((pool_size, 2 * ROWS, BLOCK), bf16),
            pltpu.VMEM((blocks, FEATS, BLOCK), bf16),
            pltpu.VMEM((max(GATHERED, capacity), entries * BLOCK, BLOCK), bf16),
            pltpu.VMEM((max(GATHERED, capacity), entries * BLOCK, BLOCK), bf16),
            pltpu.VMEM((blocks, chunks * BLOCK, BLOCK), bf16),
            pltpu.VMEM((chunks, BLOCK, FEATS), bf16),
            pltpu.VMEM((chunks, 2 * ROWS, BLOCK), bf16),
            pltpu.VMEM((2, members, 4, BLOCK), f32),
            pltpu.VMEM((2, members, 4, BLOCK), f32),
            pltpu.VMEM((2, chunks, ROWS, BLOCK), f32),
            pltpu.VMEM((2, groups, chunks, ROWS, BLOCK), f32),
            pltpu.VMEM((2, members, capacity, 4, BLOCK), f32),
            pltpu.VMEM((members, capacity, 4, BLOCK), f32),
            pltpu.VMEM((members, capacity, 4, BLOCK), f32),
            pltpu.VMEM((2, members, capacity, 3, BLOCK), f32),
            pltpu.VMEM((members, capacity, 3, BLOCK), f32),
            pltpu.VMEM((members, capacity, 3, BLOCK), f32),
            dma((9,)),
            dma((2, members)),
            dma((2, members)),
            dma((2, groups)),
            dma((2, groups)),
            dma((2, members)),
            dma((2, members)),
            dma((2, members)),
            dma((2, members)),
        ],
        compiler_params=pltpu.CompilerParams(
            collective_id=0, has_side_effects=True, vmem_limit_bytes=40 * 1024 * 1024
        ),
        name="two_steps",
    )(
        *(
            pltpu.with_memory_space_constraint(array, pltpu.HBM)
            for array in (
                position,
                velocity,
                mass.reshape(blocks, BLOCK),
                neighbours.T,
                list_length,
                let_list,
                cell_list,
                destination,
            )
        )
    )
    whole = pl.BlockSpec(memory_space=pl.ANY)
    return pl.pallas_call(
        put_out,
        out_shape=(
            jax.ShapeDtypeStruct(position.shape, f32),
            jax.ShapeDtypeStruct(velocity.shape, f32),
            jax.ShapeDtypeStruct(mass.shape, f32),
        ),
        in_specs=[vmem] * 3,
        out_specs=(whole,) * 3,
        scratch_shapes=[dma((3,))],
        compiler_params=pltpu.CompilerParams(vmem_limit_bytes=2 * 1024 * 1024),
        name="put_out",
    )(results[0], results[1], results[2].reshape(-1))


def solution(mesh):
    shared = ("group", "member")
    return jax.shard_map(
        shards,
        mesh=mesh,
        in_specs=(
            P(None, shared),
            P(None, shared),
            P(shared),
            P(shared, None),
            P(shared),
            P(shared, None),
            P(shared, None),
            P(None, shared),
        ),
        out_specs=(P(None, shared), P(None, shared), P(shared)),
        check_vma=False,
    )
```

```python
import functools
import math

import jax
import jax.numpy as jnp
from jax import lax
from jax.experimental import pallas as pl
from jax.experimental.pallas import tpu as pltpu
from jax.sharding import PartitionSpec as P

BLOCK = 128
CELL = 16
SOFTENING = 0.01
TIMESTEP = 0.1
ROWS = 8
FEATS = 64
HALF = 0.5 * TIMESTEP
GATHERED = 16


def parts_of(value):
    high = value.astype(jnp.bfloat16).astype(jnp.float32)
    rest = value - high
    middle = rest.astype(jnp.bfloat16).astype(jnp.float32)
    return high, middle, rest - middle


def rows_of(shape):
    return lax.broadcasted_iota(jnp.int32, shape, 0)


def source_features(block):
    row = rows_of(block.shape)
    mass = block[3:4]
    square = jnp.sum(jnp.where(row < 3, block * block, 0.0), axis=0, keepdims=True)
    tail = jnp.where(row == 3, square, jnp.where(row == 4, 1.0, 0.0))
    high, middle, low = parts_of(jnp.where(row < 3, block, tail))
    columns = jnp.concatenate([high, high, high, middle, middle, middle, low, low], axis=0)
    weighted = jnp.where(row < 3, block * mass, jnp.where(row == 3, mass, 0.0))
    heavy, light, least = [part[0:4] for part in parts_of(weighted)]
    moments = jnp.concatenate([heavy, light, least, jnp.zeros_like(least)], axis=0)
    return jnp.transpose(columns).astype(jnp.bfloat16), moments.astype(jnp.bfloat16)


def target_features(block):
    row = rows_of(block.shape)
    square = jnp.sum(jnp.where(row < 3, block * block, 0.0), axis=0, keepdims=True)
    tail = jnp.where(row == 3, 1.0, jnp.where(row == 4, square + SOFTENING, 0.0))
    high, middle, low = parts_of(jnp.where(row < 3, -2.0 * block, tail))
    rows = jnp.concatenate([high, middle, low, high, middle, low, high, middle], axis=0)
    return rows.astype(jnp.bfloat16)


def weights_of(radius_sq):
    inverse = lax.rsqrt(radius_sq)
    return (inverse * inverse * inverse).astype(jnp.bfloat16)


def fold(sums):
    pair = sums[0:8] + sums[8:16]
    return pair[0:4] + pair[4:8]


def migration(destination, member, members, blocks, capacity):
    lane = lax.broadcasted_iota(jnp.int32, (1, BLOCK), 1)
    spare = jnp.zeros((1, BLOCK - blocks), jnp.int32)
    shift = jnp.concatenate([destination, spare], axis=1) - member
    shift = jnp.where(shift < 0, shift + members, shift)
    shift = jnp.where(lane < blocks, shift, members)
    rows = -(-members // ROWS) * ROWS
    row = rows_of((rows, BLOCK))
    lanes = lax.broadcasted_iota(jnp.int32, (rows, BLOCK), 1)
    mine = jnp.where(row == shift, 1, 0)
    count, step = mine, 1
    while step < blocks:
        count = count + jnp.where(lanes >= step, pltpu.roll(count, step, 1), 0)
        step *= 2
    rank = jnp.sum(mine * (count - 1), axis=0, keepdims=True)
    slot = jnp.where(lane < blocks, shift * capacity + rank, -1)
    across = jnp.transpose(jnp.broadcast_to(slot, (BLOCK, BLOCK)))
    square = lax.broadcasted_iota(jnp.int32, (BLOCK, BLOCK), 1)
    order = jnp.sum(jnp.where(across == square, rows_of((BLOCK, BLOCK)), 0), axis=0, keepdims=True)
    return order, jnp.clip(slot, 0, members * capacity - 1)


def kernel(
    sizes,
    position_hbm,
    velocity_hbm,
    mass_hbm,
    neighbours_hbm,
    length_hbm,
    let_hbm,
    cell_hbm,
    destination_hbm,
    out_position,
    out_velocity,
    out_mass,
    position,
    velocity,
    mass,
    neighbours,
    lengths,
    lets,
    cells,
    destination,
    tables,
    table,
    half,
    speed,
    columns,
    moments,
    targets,
    first_weights,
    second_weights,
    far_weights,
    far_columns,
    far_moments,
    let_out,
    let_in,
    cell_out,
    cell_in,
    early_out,
    early_first,
    early_second,
    late_out,
    late_first,
    late_second,
    load_sem,
    let_send,
    let_recv,
    cell_send,
    cell_recv,
    early_send,
    early_recv,
    late_send,
    late_recv,
):
    blocks, entries, members, groups, capacity, publish = sizes
    slots = members * capacity
    chunks = far_columns.shape[0]
    per_chunk = groups // chunks
    group, member = lax.axis_index("group"), lax.axis_index("member")
    early_in, late_in = (early_first, early_second), (late_first, late_second)
    weights = (first_weights, second_weights)

    loads = [
        pltpu.make_async_copy(one, other, load_sem.at[at])
        for at, (one, other) in enumerate(
            (
                (destination_hbm, destination),
                (position_hbm, position),
                (velocity_hbm, velocity),
                (mass_hbm, mass),
                (let_hbm, lets),
                (cell_hbm, cells),
                (neighbours_hbm, neighbours),
                (length_hbm, lengths),
                (tables, table),
            )
        )
    ]
    for load in loads[:-1]:
        load.start()

    def peer(distance):
        return {"member": lax.rem(member + distance, members)}

    def group_peer(distance):
        return {"group": lax.rem(group + distance, groups)}

    mesh_id = pl.DeviceIdType.MESH
    barrier = pltpu.get_barrier_semaphore()
    for distance in range(1, members):
        pl.semaphore_signal(barrier, inc=1, device_id=peer(distance), device_id_type=mesh_id)
    for distance in range(1, groups):
        pl.semaphore_signal(barrier, inc=1, device_id=group_peer(distance), device_id_type=mesh_id)

    def let_copy(turn, distance):
        return pltpu.make_async_remote_copy(
            src_ref=let_out.at[turn, distance],
            dst_ref=let_in.at[turn, distance],
            send_sem=let_send.at[turn, distance],
            recv_sem=let_recv.at[turn, distance],
            device_id=peer(distance),
            device_id_type=mesh_id,
        )

    def cell_copy(turn, distance):
        return pltpu.make_async_remote_copy(
            src_ref=cell_out.at[turn],
            dst_ref=cell_in.at[turn, distance],
            send_sem=cell_send.at[turn, distance],
            recv_sem=cell_recv.at[turn, distance],
            device_id=group_peer(distance),
            device_id_type=mesh_id,
        )

    def early_copy(turn, distance):
        return pltpu.make_async_remote_copy(
            src_ref=early_out.at[turn, distance],
            dst_ref=early_in[turn].at[pl.ds(distance * capacity, capacity)],
            send_sem=early_send.at[turn, distance],
            recv_sem=early_recv.at[turn, distance],
            device_id=peer(distance),
            device_id_type=mesh_id,
        )

    def late_copy(turn, distance):
        return pltpu.make_async_remote_copy(
            src_ref=late_out.at[turn, distance],
            dst_ref=late_in[turn].at[pl.ds(distance * capacity, capacity)],
            send_sem=late_send.at[turn, distance],
            recv_sem=late_recv.at[turn, distance],
            device_id=peer(distance),
            device_id_type=mesh_id,
        )

    def arrived(turn, block):
        slot = table[2 * turn + 1, block]
        before, pace = early_in[turn][slot], late_in[turn][slot]
        return before[0:3] + HALF * pace, pace, before[3:4]

    def source(block, entry):
        return jnp.where(entry < lengths[block], neighbours[entry, block], blocks + members)

    route = [*range(1, members - 2), *range(members - 1, members - 3, -1)]
    together = max(1, GATHERED // capacity)
    parties = [route[first : first + together] for first in range(0, len(route), together)] + [[0]]

    half[...] = jnp.zeros_like(half)
    columns[blocks + members], moments[blocks + members] = source_features(
        jnp.zeros((ROWS, BLOCK), jnp.float32)
    )
    row = rows_of((ROWS, BLOCK))
    lane = lax.broadcasted_iota(jnp.int32, (ROWS, BLOCK), 1)

    loads[0].wait()
    for turn in range(2):
        order, slot = migration(destination[turn : turn + 1, :], member, members, blocks, capacity)
        tables[2 * turn : 2 * turn + 1, :] = order
        tables[2 * turn + 1 : 2 * turn + 2, :] = slot
    loads[-1].start()
    for load in loads[1:-1]:
        load.wait()

    for turn in range(2):

        def load_block(block, _):
            if turn == 0:
                at = pl.ds(pl.multiple_of(block * BLOCK, BLOCK), BLOCK)
                place, pace, heft = position[:, at], velocity[:, at], mass[pl.ds(block, 1), :]
            else:
                place, pace, heft = arrived(0, block)
            half[block, 0:3, :] = place + HALF * pace
            half[block, 3:4, :] = heft
            speed[block, 0:3, :] = pace
            return 0

        if turn == 0:
            lax.fori_loop(0, blocks, load_block, 0, unroll=8)
        for distance in range(members):
            listed = lets[0, lax.rem(member + distance, members)]
            into = let_out if distance else let_in
            if turn == 0:
                into[turn, distance] = half[listed, 0:4]
            else:
                place, pace, heft = arrived(0, listed)
                into[turn, distance, 0:3, :] = place + HALF * pace
                into[turn, distance, 3:4, :] = heft
        if turn == 0:
            pl.semaphore_wait(barrier, members + groups - 2)
        for distance in route:
            let_copy(turn, distance).start()
        if turn == 1:
            lax.fori_loop(0, blocks, load_block, 0, unroll=8)

        per_block = BLOCK // CELL
        lane_cell = lane // CELL
        offset = lax.rem(group, per_chunk) * publish
        found = jnp.zeros((ROWS, BLOCK), jnp.float32)
        for entry in range(publish):
            cell = cells[0, entry]
            block = half[lax.div(cell, per_block)]
            heft = block[3:4]
            weighted = jnp.where(row < 3, block * heft, block)
            inside = lane_cell == lax.rem(cell, per_block)
            total = jnp.sum(jnp.where(inside, weighted, 0.0), axis=1, keepdims=True)
            found = jnp.where(lane == offset + entry, total, found)
        held = (lane >= offset) & (lane < offset + publish)
        heft = jnp.where(held, found[3:4], 1.0)
        found = jnp.where(row < 3, found / heft, found)
        if chunks > 1:
            cell_out[turn] = jnp.zeros_like(cell_out[turn])
        cell_out[turn, group // per_chunk] = found
        for distance in range(1, groups):
            cell_copy(turn, distance).start()

        if turn == 0:
            loads[-1].wait()
        for distance in route:
            for rank in range(capacity):
                early_out[turn, distance, rank] = half[table[2 * turn, distance * capacity + rank], 0:4]
            early_copy(turn, distance).start()
        for rank in range(capacity):
            early_in[turn][rank] = half[table[2 * turn, rank], 0:4]

        def featurise(block, _):
            here = half[block]
            columns[block], moments[block] = source_features(here)
            targets[block] = target_features(here)
            return 0

        lax.fori_loop(0, blocks, featurise, 0, unroll=8)

        for distance in range(1, groups):
            cell_copy(turn, distance).wait_recv()
        for chunk in range(chunks):
            total = cell_in[turn, 1, chunk]
            for distance in range(2, groups):
                total = total + cell_in[turn, distance, chunk]
            far_columns[chunk], far_moments[chunk] = source_features(total)

        wide = math.gcd(blocks, 4 * GATHERED)

        def spread_far(step, _):
            far_rows = jnp.concatenate([far_columns[piece] for piece in range(chunks)], axis=0)
            for inner in range(wide):
                block = step * wide + inner
                far_weights[block] = weights_of(
                    jnp.dot(far_rows, targets[block], preferred_element_type=jnp.float32)
                )
            return 0

        lax.fori_loop(0, blocks // wide, spread_far, 0)

        for distance in range(1, members):
            let_copy(turn, distance).wait_recv()

        def featurise_listed(distance, _):
            spread = jnp.concatenate(
                [let_in[turn, distance], jnp.zeros((4, BLOCK), jnp.float32)], axis=0
            )
            at = blocks + lax.rem(member + members - distance, members)
            columns[at], moments[at] = source_features(spread)
            return 0

        lax.fori_loop(0, members, featurise_listed, 0, unroll=8)

        def owned(party):
            return [
                (away, rank, table[2 * turn, away * capacity + rank])
                for away in party
                for rank in range(capacity)
            ]

        def spread(party, into):
            for index, (_, _, block) in enumerate(owned(party)):
                near_columns = jnp.concatenate(
                    [columns[source(block, entry)] for entry in range(entries)], axis=0
                )
                into[index] = weights_of(
                    jnp.dot(near_columns, targets[block], preferred_element_type=jnp.float32)
                )

        def gather(party, held):
            for index, (away, rank, block) in enumerate(owned(party)):
                all_moments = jnp.concatenate(
                    [moments[source(block, entry)] for entry in range(entries)]
                    + [far_moments[piece] for piece in range(chunks)],
                    axis=1,
                )
                all_weights = jnp.concatenate([held[index], far_weights[block]], axis=0)
                sums = fold(jnp.dot(all_moments, all_weights, preferred_element_type=jnp.float32))
                here = half[block, 0:3]
                pull = sums[0:3] - here * sums[3:4]
                pace = speed[block, 0:3] + TIMESTEP * pull
                if away:
                    late_out[turn, away, rank] = pace
                else:
                    late_in[turn][rank] = pace

        def both(ahead, behind, parity):
            spread(ahead, weights[1 - parity])
            gather(behind, weights[parity])

        spread(parties[0], weights[0])
        for at, party in enumerate(parties[:-2]):
            both(parties[at + 1], party, at % 2)
            for away in party:
                late_copy(turn, away).start()
        held = weights[(len(parties) - 2) % 2]
        gather(parties[-2], held)
        for away in parties[-2]:
            late_copy(turn, away).start()
        spread(parties[-1], held)
        gather(parties[-1], held)
        for distance in range(1, groups):
            cell_copy(turn, distance).wait_send()
        for distance in route:
            let_copy(turn, distance).wait_send()
            early_copy(turn, distance).wait_send()
            late_copy(turn, distance).wait_send()
        for distance in range(1, members):
            early_copy(turn, distance).wait_recv()
            late_copy(turn, distance).wait_recv()

    def unload(block, _):
        at = pl.ds(pl.multiple_of(block * BLOCK, BLOCK), BLOCK)
        out_position[:, at], out_velocity[:, at], out_mass[pl.ds(block, 1), :] = arrived(1, block)
        return 0

    lax.fori_loop(0, blocks, unload, 0, unroll=8)

def put_out(position, velocity, mass, final_position, final_velocity, final_mass, sent):
    pairs = ((position, final_position), (velocity, final_velocity), (mass, final_mass))
    copies = [pltpu.make_async_copy(one, other, sent.at[at]) for at, (one, other) in enumerate(pairs)]
    for copy in copies:
        copy.start()
    for copy in copies:
        copy.wait()


def shards(position, velocity, mass, neighbours, list_length, let_list, cell_list, destination):
    members, groups = lax.axis_size("member"), lax.axis_size("group")
    member = lax.axis_index("member")
    blocks, entries = neighbours.shape
    publish = cell_list.shape[1]
    capacity = (blocks + members - 1) // members
    chunks = max(1, groups * publish // BLOCK)
    vmem = pl.BlockSpec(memory_space=pltpu.VMEM)
    f32, bf16 = jnp.float32, jnp.bfloat16
    pool_size = blocks + members + 1
    dma = pltpu.SemaphoreType.DMA
    results = pl.pallas_call(
        functools.partial(kernel, (blocks, entries, members, groups, capacity, publish)),
        out_shape=(
            jax.ShapeDtypeStruct(position.shape, f32),
            jax.ShapeDtypeStruct(velocity.shape, f32),
            jax.ShapeDtypeStruct((blocks, BLOCK), f32),
        ),
        in_specs=[pl.BlockSpec(memory_space=pltpu.HBM)] * 8,
        out_specs=(vmem, vmem, vmem),
        scratch_shapes=[
            pltpu.VMEM(position.shape, f32),
            pltpu.VMEM(velocity.shape, f32),
            pltpu.VMEM((blocks, BLOCK), f32),
            pltpu.SMEM((entries, blocks), jnp.int32),
            pltpu.SMEM(list_length.shape, jnp.int32),
            pltpu.SMEM(let_list.shape, jnp.int32),
            pltpu.SMEM(cell_list.shape, jnp.int32),
            pltpu.VMEM(destination.shape, jnp.int32),
            pltpu.VMEM((4, BLOCK), jnp.int32),
            pltpu.SMEM((4, BLOCK), jnp.int32),
            pltpu.VMEM((blocks, ROWS, BLOCK), f32),
            pltpu.VMEM((blocks, ROWS, BLOCK), f32),
            pltpu.VMEM((pool_size, BLOCK, FEATS), bf16),
            pltpu.VMEM((pool_size, 2 * ROWS, BLOCK), bf16),
            pltpu.VMEM((blocks, FEATS, BLOCK), bf16),
            pltpu.VMEM((max(GATHERED, capacity), entries * BLOCK, BLOCK), bf16),
            pltpu.VMEM((max(GATHERED, capacity), entries * BLOCK, BLOCK), bf16),
            pltpu.VMEM((blocks, chunks * BLOCK, BLOCK), bf16),
            pltpu.VMEM((chunks, BLOCK, FEATS), bf16),
            pltpu.VMEM((chunks, 2 * ROWS, BLOCK), bf16),
            pltpu.VMEM((2, members, 4, BLOCK), f32),
            pltpu.VMEM((2, members, 4, BLOCK), f32),
            pltpu.VMEM((2, chunks, ROWS, BLOCK), f32),
            pltpu.VMEM((2, groups, chunks, ROWS, BLOCK), f32),
            pltpu.VMEM((2, members, capacity, 4, BLOCK), f32),
            pltpu.VMEM((members * capacity, 4, BLOCK), f32),
            pltpu.VMEM((members * capacity, 4, BLOCK), f32),
            pltpu.VMEM((2, members, capacity, 3, BLOCK), f32),
            pltpu.VMEM((members * capacity, 3, BLOCK), f32),
            pltpu.VMEM((members * capacity, 3, BLOCK), f32),
            dma((9,)),
            dma((2, members)),
            dma((2, members)),
            dma((2, groups)),
            dma((2, groups)),
            dma((2, members)),
            dma((2, members)),
            dma((2, members)),
            dma((2, members)),
        ],
        compiler_params=pltpu.CompilerParams(
            collective_id=0, has_side_effects=True, vmem_limit_bytes=40 * 1024 * 1024
        ),
        name="two_steps",
    )(
        *(
            pltpu.with_memory_space_constraint(array, pltpu.HBM)
            for array in (
                position,
                velocity,
                mass.reshape(blocks, BLOCK),
                neighbours.T,
                list_length,
                let_list,
                cell_list,
                destination,
            )
        )
    )
    whole = pl.BlockSpec(memory_space=pl.ANY)
    return pl.pallas_call(
        put_out,
        out_shape=(
            jax.ShapeDtypeStruct(position.shape, f32),
            jax.ShapeDtypeStruct(velocity.shape, f32),
            jax.ShapeDtypeStruct(mass.shape, f32),
        ),
        in_specs=[vmem] * 3,
        out_specs=(whole,) * 3,
        scratch_shapes=[dma((3,))],
        compiler_params=pltpu.CompilerParams(vmem_limit_bytes=2 * 1024 * 1024),
        name="put_out",
    )(results[0], results[1], results[2].reshape(-1))


def solution(mesh):
    shared = ("group", "member")
    return jax.shard_map(
        shards,
        mesh=mesh,
        in_specs=(
            P(None, shared),
            P(None, shared),
            P(shared),
            P(shared, None),
            P(shared),
            P(shared, None),
            P(shared, None),
            P(None, shared),
        ),
        out_specs=(P(None, shared), P(None, shared), P(shared)),
        check_vma=False,
    )
```

```python
import functools
import math

import jax
import jax.numpy as jnp
from jax import lax
from jax.experimental import pallas as pl
from jax.experimental.pallas import tpu as pltpu
from jax.sharding import PartitionSpec as P

BLOCK = 128
CELL = 16
CELL_SHIFT = 3
SOFTENING = 0.01
TIMESTEP = 0.1
ROWS = 8
FEATS = 64
HALF = 0.5 * TIMESTEP
GATHERED = 16


def parts_of(value):
    high = value.astype(jnp.bfloat16).astype(jnp.float32)
    rest = value - high
    middle = rest.astype(jnp.bfloat16).astype(jnp.float32)
    return high, middle, rest - middle


def rows_of(shape):
    return lax.broadcasted_iota(jnp.int32, shape, 0)


def source_features(block):
    row = rows_of(block.shape)
    mass = block[3:4]
    square = jnp.sum(jnp.where(row < 3, block * block, 0.0), axis=0, keepdims=True)
    tail = jnp.where(row == 3, square, jnp.where(row == 4, 1.0, 0.0))
    high, middle, low = parts_of(jnp.where(row < 3, block, tail))
    columns = jnp.concatenate([high, high, high, middle, middle, middle, low, low], axis=0)
    weighted = jnp.where(row < 3, block * mass, jnp.where(row == 3, mass, 0.0))
    heavy, light, least = [part[0:4] for part in parts_of(weighted)]
    moments = jnp.concatenate([heavy, light, least, jnp.zeros_like(least)], axis=0)
    return jnp.transpose(columns).astype(jnp.bfloat16), moments.astype(jnp.bfloat16)


def target_features(block):
    row = rows_of(block.shape)
    square = jnp.sum(jnp.where(row < 3, block * block, 0.0), axis=0, keepdims=True)
    tail = jnp.where(row == 3, 1.0, jnp.where(row == 4, square + SOFTENING, 0.0))
    high, middle, low = parts_of(jnp.where(row < 3, -2.0 * block, tail))
    rows = jnp.concatenate([high, middle, low, high, middle, low, high, middle], axis=0)
    return rows.astype(jnp.bfloat16)


def weights_of(radius_sq):
    inverse = lax.rsqrt(radius_sq)
    return (inverse * inverse * inverse).astype(jnp.bfloat16)


def fold(sums):
    pair = sums[0:8] + sums[8:16]
    return pair[0:4] + pair[4:8]


def migration(destination, member, members, blocks, capacity):
    lane = lax.broadcasted_iota(jnp.int32, (1, BLOCK), 1)
    spare = jnp.zeros((1, BLOCK - blocks), jnp.int32)
    shift = jnp.concatenate([destination, spare], axis=1) - member
    shift = jnp.where(shift < 0, shift + members, shift)
    shift = jnp.where(lane < blocks, shift, members)
    rows = -(-members // ROWS) * ROWS
    row = rows_of((rows, BLOCK))
    lanes = lax.broadcasted_iota(jnp.int32, (rows, BLOCK), 1)
    mine = jnp.where(row == shift, 1, 0)
    count, step = mine, 1
    while step < blocks:
        count = count + jnp.where(lanes >= step, pltpu.roll(count, step, 1), 0)
        step *= 2
    rank = jnp.sum(mine * (count - 1), axis=0, keepdims=True)
    slot = jnp.where(lane < blocks, shift * capacity + rank, -1)
    across = jnp.transpose(jnp.broadcast_to(slot, (BLOCK, BLOCK)))
    square = lax.broadcasted_iota(jnp.int32, (BLOCK, BLOCK), 1)
    order = jnp.sum(jnp.where(across == square, rows_of((BLOCK, BLOCK)), 0), axis=0, keepdims=True)
    return order, jnp.clip(slot, 0, members * capacity - 1)


def kernel(
    sizes,
    position_hbm,
    velocity_hbm,
    mass_hbm,
    neighbours_hbm,
    length_hbm,
    let_hbm,
    cell_hbm,
    destination_hbm,
    out_position,
    out_velocity,
    out_mass,
    position,
    velocity,
    mass,
    neighbours,
    lengths,
    lets,
    cells,
    destination,
    tables,
    table,
    half,
    speed,
    columns,
    moments,
    targets,
    first_weights,
    second_weights,
    far_weights,
    far_columns,
    far_moments,
    let_out,
    let_in,
    cell_out,
    cell_in,
    early_out,
    early_first,
    early_second,
    late_out,
    late_first,
    late_second,
    load_sem,
    let_send,
    let_recv,
    cell_send,
    cell_recv,
    early_send,
    early_recv,
    late_send,
    late_recv,
):
    blocks, entries, members, groups, capacity, publish = sizes
    slots = members * capacity
    chunks = far_columns.shape[0]
    per_chunk = groups // chunks
    group, member = lax.axis_index("group"), lax.axis_index("member")
    early_in, late_in = (early_first, early_second), (late_first, late_second)
    weights = (first_weights, second_weights)

    loads = [
        pltpu.make_async_copy(one, other, load_sem.at[at])
        for at, (one, other) in enumerate(
            (
                (destination_hbm, destination),
                (position_hbm, position),
                (velocity_hbm, velocity),
                (mass_hbm, mass),
                (let_hbm, lets),
                (cell_hbm, cells),
                (neighbours_hbm, neighbours),
                (length_hbm, lengths),
                (tables, table),
            )
        )
    ]
    for load in loads[:-1]:
        load.start()

    def peer(distance):
        return {"member": lax.rem(member + distance, members)}

    def group_peer(distance):
        return {"group": lax.rem(group + distance, groups)}

    mesh_id = pl.DeviceIdType.MESH
    barrier = pltpu.get_barrier_semaphore()
    for distance in range(1, members):
        pl.semaphore_signal(barrier, inc=1, device_id=peer(distance), device_id_type=mesh_id)
    for distance in range(1, groups):
        pl.semaphore_signal(barrier, inc=1, device_id=group_peer(distance), device_id_type=mesh_id)

    def let_copy(turn, distance):
        return pltpu.make_async_remote_copy(
            src_ref=let_out.at[turn, distance],
            dst_ref=let_in.at[turn, distance],
            send_sem=let_send.at[turn],
            recv_sem=let_recv.at[turn],
            device_id=peer(distance),
            device_id_type=mesh_id,
        )

    def cell_copy(turn, distance):
        return pltpu.make_async_remote_copy(
            src_ref=cell_out.at[turn],
            dst_ref=cell_in.at[turn, distance],
            send_sem=cell_send.at[turn],
            recv_sem=cell_recv.at[turn],
            device_id=group_peer(distance),
            device_id_type=mesh_id,
        )

    def early_copy(turn, distance):
        return pltpu.make_async_remote_copy(
            src_ref=early_out.at[turn, distance],
            dst_ref=early_in[turn].at[pl.ds(distance * capacity, capacity)],
            send_sem=early_send.at[turn],
            recv_sem=early_recv.at[turn],
            device_id=peer(distance),
            device_id_type=mesh_id,
        )

    def late_copy(turn, distance):
        return pltpu.make_async_remote_copy(
            src_ref=late_out.at[turn, distance],
            dst_ref=late_in[turn].at[pl.ds(distance * capacity, capacity)],
            send_sem=late_send.at[turn],
            recv_sem=late_recv.at[turn],
            device_id=peer(distance),
            device_id_type=mesh_id,
        )

    def await_bytes(ref, sem):
        pltpu.make_async_copy(ref, ref, sem).wait()

    def arrived(turn, block):
        slot = table[2 * turn + 1, block]
        before, pace = early_in[turn][slot], late_in[turn][slot]
        return before[0:3] + HALF * pace, pace, before[3:4]

    def source(block, entry):
        return jnp.where(entry < lengths[block], neighbours[entry, block], blocks + members)

    route = [*range(1, members - 2), *range(members - 1, members - 3, -1)]
    together = max(1, GATHERED // capacity)
    parties = [route[first : first + together] for first in range(0, len(route), together)] + [[0]]

    half[...] = jnp.zeros_like(half)
    columns[blocks + members], moments[blocks + members] = source_features(
        jnp.zeros((ROWS, BLOCK), jnp.float32)
    )
    row = rows_of((ROWS, BLOCK))
    lane = lax.broadcasted_iota(jnp.int32, (ROWS, BLOCK), 1)

    loads[0].wait()
    for turn in range(2):
        order, slot = migration(destination[turn : turn + 1, :], member, members, blocks, capacity)
        tables[2 * turn : 2 * turn + 1, :] = order
        tables[2 * turn + 1 : 2 * turn + 2, :] = slot
    loads[-1].start()
    for load in loads[1:-1]:
        load.wait()

    for turn in range(2):

        def load_block(block, _):
            if turn == 0:
                at = pl.ds(pl.multiple_of(block * BLOCK, BLOCK), BLOCK)
                place, pace, heft = position[:, at], velocity[:, at], mass[pl.ds(block, 1), :]
            else:
                place, pace, heft = arrived(0, block)
            half[block, 0:3, :] = place + HALF * pace
            half[block, 3:4, :] = heft
            speed[block, 0:3, :] = pace
            return 0

        if turn == 0:
            lax.fori_loop(0, blocks, load_block, 0, unroll=8)
        for distance in range(members):
            listed = lets[0, lax.rem(member + distance, members)]
            into = let_out if distance else let_in
            if turn == 0:
                into[turn, distance] = half[listed, 0:4]
            else:
                place, pace, heft = arrived(0, listed)
                into[turn, distance, 0:3, :] = place + HALF * pace
                into[turn, distance, 3:4, :] = heft
        if turn == 0:
            pl.semaphore_wait(barrier, members + groups - 2)
        for distance in route:
            let_copy(turn, distance).start()
        if turn == 1:
            lax.fori_loop(0, blocks, load_block, 0, unroll=8)

        per_block = BLOCK // CELL
        assert per_block == 1 << CELL_SHIFT
        lane_cell = lane // CELL
        offset = lax.rem(group, per_chunk) * publish
        found = jnp.zeros((ROWS, BLOCK), jnp.float32)
        for entry in range(publish):
            cell = cells[0, entry]
            block = half[lax.shift_right_logical(cell, CELL_SHIFT)]
            heft = block[3:4]
            weighted = jnp.where(row < 3, block * heft, block)
            inside = lane_cell == lax.bitwise_and(cell, per_block - 1)
            total = jnp.sum(jnp.where(inside, weighted, 0.0), axis=1, keepdims=True)
            found = jnp.where(lane == offset + entry, total, found)
        held = (lane >= offset) & (lane < offset + publish)
        heft = jnp.where(held, found[3:4], 1.0)
        found = jnp.where(row < 3, found / heft, found)
        if chunks > 1:
            cell_out[turn] = jnp.zeros_like(cell_out[turn])
        cell_out[turn, group // per_chunk] = found
        for distance in range(1, groups):
            cell_copy(turn, distance).start()

        if turn == 0:
            loads[-1].wait()
        for distance in route:
            for rank in range(capacity):
                early_out[turn, distance, rank] = half[table[2 * turn, distance * capacity + rank], 0:4]
            early_copy(turn, distance).start()
        for rank in range(capacity):
            early_in[turn][rank] = half[table[2 * turn, rank], 0:4]

        def featurise(block, _):
            here = half[block]
            columns[block], moments[block] = source_features(here)
            targets[block] = target_features(here)
            return 0

        lax.fori_loop(0, blocks, featurise, 0, unroll=8)

        await_bytes(cell_in.at[turn, pl.ds(1, groups - 1)], cell_recv.at[turn])
        for chunk in range(chunks):
            total = cell_in[turn, 1, chunk]
            for distance in range(2, groups):
                total = total + cell_in[turn, distance, chunk]
            far_columns[chunk], far_moments[chunk] = source_features(total)

        wide = math.gcd(blocks, 4 * GATHERED)

        def spread_far(step, _):
            far_rows = jnp.concatenate([far_columns[piece] for piece in range(chunks)], axis=0)
            for inner in range(wide):
                block = step * wide + inner
                far_weights[block] = weights_of(
                    jnp.dot(far_rows, targets[block], preferred_element_type=jnp.float32)
                )
            return 0

        lax.fori_loop(0, blocks // wide, spread_far, 0)

        await_bytes(let_in.at[turn, pl.ds(1, members - 1)], let_recv.at[turn])

        def featurise_listed(distance, _):
            spread = jnp.concatenate(
                [let_in[turn, distance], jnp.zeros((4, BLOCK), jnp.float32)], axis=0
            )
            at = blocks + lax.rem(member + members - distance, members)
            columns[at], moments[at] = source_features(spread)
            return 0

        lax.fori_loop(0, members, featurise_listed, 0, unroll=8)

        def owned(party):
            return [
                (away, rank, table[2 * turn, away * capacity + rank])
                for away in party
                for rank in range(capacity)
            ]

        def spread(party, into):
            for index, (_, _, block) in enumerate(owned(party)):
                near_columns = jnp.concatenate(
                    [columns[source(block, entry)] for entry in range(entries)], axis=0
                )
                into[index] = weights_of(
                    jnp.dot(near_columns, targets[block], preferred_element_type=jnp.float32)
                )

        def gather(party, held):
            for index, (away, rank, block) in enumerate(owned(party)):
                all_moments = jnp.concatenate(
                    [moments[source(block, entry)] for entry in range(entries)]
                    + [far_moments[piece] for piece in range(chunks)],
                    axis=1,
                )
                all_weights = jnp.concatenate([held[index], far_weights[block]], axis=0)
                sums = fold(jnp.dot(all_moments, all_weights, preferred_element_type=jnp.float32))
                here = half[block, 0:3]
                pull = sums[0:3] - here * sums[3:4]
                pace = speed[block, 0:3] + TIMESTEP * pull
                if away:
                    late_out[turn, away, rank] = pace
                else:
                    late_in[turn][rank] = pace

        def both(ahead, behind, parity):
            spread(ahead, weights[1 - parity])
            gather(behind, weights[parity])

        spread(parties[0], weights[0])
        for at, party in enumerate(parties[:-2]):
            both(parties[at + 1], party, at % 2)
            for away in party:
                late_copy(turn, away).start()
        held = weights[(len(parties) - 2) % 2]
        gather(parties[-2], held)
        for away in parties[-2]:
            late_copy(turn, away).start()
        spread(parties[-1], held)
        gather(parties[-1], held)
        await_bytes(cell_in.at[turn, pl.ds(1, groups - 1)], cell_send.at[turn])
        await_bytes(let_out.at[turn, pl.ds(1, members - 1)], let_send.at[turn])
        await_bytes(early_out.at[turn, pl.ds(1, members - 1)], early_send.at[turn])
        await_bytes(late_out.at[turn, pl.ds(1, members - 1)], late_send.at[turn])
        landed = pl.ds(capacity, (members - 1) * capacity)
        await_bytes(early_in[turn].at[landed], early_recv.at[turn])
        await_bytes(late_in[turn].at[landed], late_recv.at[turn])

    def unload(block, _):
        at = pl.ds(pl.multiple_of(block * BLOCK, BLOCK), BLOCK)
        out_position[:, at], out_velocity[:, at], out_mass[pl.ds(block, 1), :] = arrived(1, block)
        return 0

    lax.fori_loop(0, blocks, unload, 0, unroll=8)

def put_out(position, velocity, mass, final_position, final_velocity, final_mass, sent):
    pairs = ((position, final_position), (velocity, final_velocity), (mass, final_mass))
    copies = [pltpu.make_async_copy(one, other, sent.at[at]) for at, (one, other) in enumerate(pairs)]
    for copy in copies:
        copy.start()
    for copy in copies:
        copy.wait()


def shards(position, velocity, mass, neighbours, list_length, let_list, cell_list, destination):
    members, groups = lax.axis_size("member"), lax.axis_size("group")
    member = lax.axis_index("member")
    blocks, entries = neighbours.shape
    publish = cell_list.shape[1]
    capacity = (blocks + members - 1) // members
    chunks = max(1, groups * publish // BLOCK)
    vmem = pl.BlockSpec(memory_space=pltpu.VMEM)
    f32, bf16 = jnp.float32, jnp.bfloat16
    pool_size = blocks + members + 1
    dma = pltpu.SemaphoreType.DMA
    results = pl.pallas_call(
        functools.partial(kernel, (blocks, entries, members, groups, capacity, publish)),
        out_shape=(
            jax.ShapeDtypeStruct(position.shape, f32),
            jax.ShapeDtypeStruct(velocity.shape, f32),
            jax.ShapeDtypeStruct((blocks, BLOCK), f32),
        ),
        in_specs=[pl.BlockSpec(memory_space=pltpu.HBM)] * 8,
        out_specs=(vmem, vmem, vmem),
        scratch_shapes=[
            pltpu.VMEM(position.shape, f32),
            pltpu.VMEM(velocity.shape, f32),
            pltpu.VMEM((blocks, BLOCK), f32),
            pltpu.SMEM((entries, blocks), jnp.int32),
            pltpu.SMEM(list_length.shape, jnp.int32),
            pltpu.SMEM(let_list.shape, jnp.int32),
            pltpu.SMEM(cell_list.shape, jnp.int32),
            pltpu.VMEM(destination.shape, jnp.int32),
            pltpu.VMEM((4, BLOCK), jnp.int32),
            pltpu.SMEM((4, BLOCK), jnp.int32),
            pltpu.VMEM((blocks, ROWS, BLOCK), f32),
            pltpu.VMEM((blocks, ROWS, BLOCK), f32),
            pltpu.VMEM((pool_size, BLOCK, FEATS), bf16),
            pltpu.VMEM((pool_size, 2 * ROWS, BLOCK), bf16),
            pltpu.VMEM((blocks, FEATS, BLOCK), bf16),
            pltpu.VMEM((max(GATHERED, capacity), entries * BLOCK, BLOCK), bf16),
            pltpu.VMEM((max(GATHERED, capacity), entries * BLOCK, BLOCK), bf16),
            pltpu.VMEM((blocks, chunks * BLOCK, BLOCK), bf16),
            pltpu.VMEM((chunks, BLOCK, FEATS), bf16),
            pltpu.VMEM((chunks, 2 * ROWS, BLOCK), bf16),
            pltpu.VMEM((2, members, 4, BLOCK), f32),
            pltpu.VMEM((2, members, 4, BLOCK), f32),
            pltpu.VMEM((2, chunks, ROWS, BLOCK), f32),
            pltpu.VMEM((2, groups, chunks, ROWS, BLOCK), f32),
            pltpu.VMEM((2, members, capacity, 4, BLOCK), f32),
            pltpu.VMEM((members * capacity, 4, BLOCK), f32),
            pltpu.VMEM((members * capacity, 4, BLOCK), f32),
            pltpu.VMEM((2, members, capacity, 3, BLOCK), f32),
            pltpu.VMEM((members * capacity, 3, BLOCK), f32),
            pltpu.VMEM((members * capacity, 3, BLOCK), f32),
            dma((9,)),
            dma((2,)),
            dma((2,)),
            dma((2,)),
            dma((2,)),
            dma((2,)),
            dma((2,)),
            dma((2,)),
            dma((2,)),
        ],
        compiler_params=pltpu.CompilerParams(
            collective_id=0, has_side_effects=True, vmem_limit_bytes=40 * 1024 * 1024
        ),
        name="two_steps",
    )(
        *(
            pltpu.with_memory_space_constraint(array, pltpu.HBM)
            for array in (
                position,
                velocity,
                mass.reshape(blocks, BLOCK),
                neighbours.T,
                list_length,
                let_list,
                cell_list,
                destination,
            )
        )
    )
    whole = pl.BlockSpec(memory_space=pl.ANY)
    return pl.pallas_call(
        put_out,
        out_shape=(
            jax.ShapeDtypeStruct(position.shape, f32),
            jax.ShapeDtypeStruct(velocity.shape, f32),
            jax.ShapeDtypeStruct(mass.shape, f32),
        ),
        in_specs=[vmem] * 3,
        out_specs=(whole,) * 3,
        scratch_shapes=[dma((3,))],
        compiler_params=pltpu.CompilerParams(vmem_limit_bytes=2 * 1024 * 1024),
        name="put_out",
    )(results[0], results[1], results[2].reshape(-1))


def solution(mesh):
    shared = ("group", "member")
    return jax.shard_map(
        shards,
        mesh=mesh,
        in_specs=(
            P(None, shared),
            P(None, shared),
            P(shared),
            P(shared, None),
            P(shared),
            P(shared, None),
            P(shared, None),
            P(None, shared),
        ),
        out_specs=(P(None, shared), P(None, shared), P(shared)),
        check_vma=False,
    )
```
